32 devices in a mesh: slab: 4 (over x, core), energy: 8 (over z, y).
Axes of the slice: x: 2, y: 2, z: 4, core: 2. Of those that a mesh axis runs over, the one named last changes fastest.
Arguments:
- onsite: float32 [4, 384], P('slab'), may hold values from -1 to 1
- hopping: float32 [4, 384, 384], P('slab'), may hold values from -0.09 to 0.09, as said below
- separator_hamiltonian: float32 [128, 128], replicated, may hold values from -1 to 1, as said below
- coupling: float32 [4, 128], P('slab'), may hold values from 0.3 to 0.8
- bound_rows: int32 [4, 128], P('slab'), may hold values from 0 to 383, as said below
- old_sigma: float32 [2, 8, 4, 384, 384], P(None, 'energy', 'slab'), may hold values from -0.125 to 0.125
- phonon_vertex: float32 [4, 384, 384], P('slab'), may hold values from -0.3125 to 0.3125
- mode_steps: int32 [2], replicated, may hold values from 1 to 2, as said below
- mode_weights: float32 [2, 2], replicated, may hold values from 0.3 to 3
Outputs:
- new_sigma: float32 [2, 8, 4, 384, 384], P(None, 'energy', 'slab')
The draws below stay inside these ranges and needn't reach their ends.
Inputs may be any that keep to these rules, and one draw needn't show every extreme that they name: Each slab's hopping block is symmetric with a zero diagonal. `separator_hamiltonian`: symmetric. `bound_rows`: each slab's 128 entries are distinct and ascending and include the slab's first and last orbital. `mode_steps`: the 2 modes have distinct steps.
All inputs are finite; a program needn't handle non-finite values.
Results may differ from the reference program's by a relative error of at most 0.0001.
Values sent between devices are 32-bit elements; how exact they have to be, the bound alone decides.
No kernel may reach another device: no remote copies, remote signals or barrier semaphores. Data moves between devices by JAX's collectives and lax.ppermute only.
A program may use at most 192 MiB of HBM per device.

```python
import math
import jax
import jax.numpy as jnp
from jax import lax

SLAB = 384
SEP = 128
ITERS = 3
MODES = 2
SLABS = 4
ENERGIES = 8


def symmetric_block(key, count, order_size, scale):
    raw = jnp.clip(jax.random.normal(key, (count, order_size, order_size), jnp.float32), -4.0, 4.0)
    mirrored = (raw + jnp.swapaxes(raw, -1, -2)) * (scale / math.sqrt(2.0))
    return mirrored * (1.0 - jnp.eye(order_size, dtype=jnp.float32))


def draw_hopping(key, part):
    return symmetric_block(jax.random.fold_in(key, 11), SLABS, SLAB, 0.015)


def draw_separator_hamiltonian(key, part):
    offdiag = symmetric_block(jax.random.fold_in(key, 23), 1, SEP, 0.015)[0]
    levels = jax.random.uniform(jax.random.fold_in(key, 29), (SEP,), jnp.float32, -1.0, 1.0)
    return offdiag + jnp.diag(levels)


def draw_bound_rows(key, part):
    keys = jax.random.split(jax.random.fold_in(key, 37), SLABS)

    def one_slab(slab_key):
        inner = jax.random.permutation(slab_key, SLAB - 2).astype(jnp.int32) + 1
        chosen = jnp.concatenate([jnp.zeros((1,), jnp.int32), inner[:SEP - 2], jnp.full((1,), SLAB - 1, jnp.int32)])
        return jnp.sort(chosen)
    return jax.vmap(one_slab)(keys).astype(jnp.int32)


def draw_mode_steps(key, part):
    return (jax.random.permutation(jax.random.fold_in(key, 41), MODES).astype(jnp.int32) + 1).astype(jnp.int32)


def steps_of(key, extent, shards, least, top_value):
    factor_of = 1.0
    for axis_at, parts in shards:
        heights = jax.random.uniform(jax.random.fold_in(jax.random.fold_in(key, 6), axis_at), (parts,), jnp.float32, least / len(shards), top_value / len(shards))
        factor_of = factor_of * jnp.repeat(jnp.exp(heights), extent[axis_at] // parts).reshape((-1,) + (1,) * (len(extent) - 1 - axis_at))
    return factor_of


def centred(key, extent, spread, limit, cuts=(), kind=jnp.bfloat16):
    drawn = jax.random.normal(key, extent, jnp.float32) * spread
    if len(cuts) > 0:
        drawn = steps_of(key, extent, cuts, -0.22, 0.18) * drawn
    return jnp.clip(drawn, min=-limit, max=limit).astype(kind)


def setup_inputs(seed: int = 0) -> dict:
    streams_of = jax.random.split(jax.random.key(seed), 10)
    onsite = jnp.clip(jax.random.uniform(streams_of[0], (SLABS, SLAB), jnp.float32, -1.0, 1.0) * steps_of(streams_of[0], (SLABS, SLAB), ((0, 4),), -0.4, 0.0), -1.0, 1.0)
    hopping = draw_hopping(jax.random.fold_in(streams_of[9], 71), 0)
    separator_hamiltonian = draw_separator_hamiltonian(jax.random.fold_in(streams_of[9], 71), 0)
    coupling = jnp.clip(0.3 + 0.5 * jax.random.uniform(streams_of[3], (SLABS, SEP), jnp.float32) ** steps_of(streams_of[3], (SLABS, SEP), ((0, 4),), -0.2, 0.2), 0.3, 0.8)
    bound_rows = draw_bound_rows(jax.random.fold_in(streams_of[9], 71), 0)
    old_sigma = centred(streams_of[5], (2, ENERGIES, SLABS, SLAB, SLAB), 0.008, 0.125, ((1, 8), (2, 4)), jnp.float32)
    phonon_vertex = centred(streams_of[6], (SLABS, SLAB, SLAB), SLAB ** -0.5, 0.3125, ((0, 4),), jnp.float32)
    mode_steps = draw_mode_steps(jax.random.fold_in(streams_of[9], 71), 0)
    mode_weights = jnp.clip(jnp.exp(jax.random.uniform(streams_of[8], (2, MODES), jnp.float32, math.log(0.3), math.log(3.0))), 0.3, 3.0)
    return {"onsite": onsite, "hopping": hopping, "separator_hamiltonian": separator_hamiltonian, "coupling": coupling, "bound_rows": bound_rows, "old_sigma": old_sigma, "phonon_vertex": phonon_vertex, "mode_steps": mode_steps, "mode_weights": mode_weights}


BROADENING = 1.0
LOWEST = -2.0
SPREAD = 4.0


def complex_product(former, latter):
    highest = lax.Precision.HIGHEST
    real_part = jnp.matmul(former[0], latter[0], precision=highest) - jnp.matmul(former[1], latter[1], precision=highest)
    imaginary = jnp.matmul(former[0], latter[1], precision=highest) + jnp.matmul(former[1], latter[0], precision=highest)
    return jnp.stack([real_part, imaginary])


def complex_scale(former, latter):
    real_part = former[0] * latter[0] - former[1] * latter[1]
    imaginary = former[0] * latter[1] + former[1] * latter[0]
    return jnp.stack([real_part, imaginary])


def refine(matrix):
    order_size = matrix.shape[-1]
    identity = jnp.eye(order_size, dtype=jnp.float32)
    diagonal = jnp.diagonal(matrix, axis1=-2, axis2=-1)
    magnitude = diagonal[0] * diagonal[0] + diagonal[1] * diagonal[1]
    start = jnp.stack([diagonal[0] / magnitude, -diagonal[1] / magnitude])
    first = complex_scale(complex_scale(start[..., :, None], matrix), start[..., None, :])
    estimate = 2.0 * identity * start[..., None, :] - first
    for repeat in range(ITERS - 1):
        product = complex_product(matrix, estimate)
        correction = jnp.stack([2.0 * identity - product[0], -product[1]])
        estimate = complex_product(estimate, correction)
    return estimate


def green_blocks(sigma_one, energy_value, onsite, hopping, separator_hamiltonian, coupling, bound_rows):
    order_size = hopping.shape[-1]
    identity = jnp.eye(order_size, dtype=jnp.float32)
    real_part = energy_value * identity - hopping - onsite[:, :, None] * identity - sigma_one[0]
    imaginary = BROADENING * identity - sigma_one[1]
    slab_inverse = refine(jnp.stack([real_part, imaginary]))
    picked = jnp.take_along_axis(slab_inverse, bound_rows[None, :, None, :], axis=3)
    corner = jnp.take_along_axis(picked, bound_rows[None, :, :, None], axis=2)
    weighted = corner * coupling[None, :, :, None] * coupling[None, :, None, :]
    schur = jnp.sum(weighted, axis=1)
    sep_identity = jnp.eye(separator_hamiltonian.shape[0], dtype=jnp.float32)
    separator = jnp.stack([energy_value * sep_identity - separator_hamiltonian - schur[0], BROADENING * sep_identity - schur[1]])
    separator_inverse = refine(separator)
    columns = picked * coupling[None, :, None, :]
    rows_part = jnp.take_along_axis(slab_inverse, bound_rows[None, :, :, None], axis=2) * coupling[None, :, :, None]
    middle = complex_product(columns, separator_inverse[:, None])
    return slab_inverse + complex_product(middle, rows_part)


def offset_weights(mode_steps, mode_weights):
    distances = jnp.arange(1, 3, dtype=jnp.int32)
    matched = (mode_steps[None, :] == distances[:, None]).astype(jnp.float32)
    absorb = jnp.sum(matched * mode_weights[0][None, :], axis=1)
    emit = jnp.sum(matched * mode_weights[1][None, :], axis=1)
    return absorb, emit


def reference(onsite, hopping, separator_hamiltonian, coupling, bound_rows, old_sigma, phonon_vertex, mode_steps, mode_weights):
    energy_count = old_sigma.shape[1]

    def one_energy(packed):
        sigma_one, energy_index = packed
        energy_value = LOWEST + SPREAD * (energy_index.astype(jnp.float32) + 0.5) / energy_count
        return green_blocks(sigma_one, energy_value, onsite, hopping, separator_hamiltonian, coupling, bound_rows)

    greens = lax.map(one_energy, (jnp.moveaxis(old_sigma, 1, 0), jnp.arange(energy_count, dtype=jnp.int32)))
    absorb, emit = offset_weights(mode_steps, mode_weights)
    mixed = jnp.zeros_like(greens)
    for distance in (1, 2):
        lower = jnp.concatenate([jnp.zeros_like(greens[:distance]), greens[:-distance]], axis=0)
        upper = jnp.concatenate([greens[distance:], jnp.zeros_like(greens[:distance])], axis=0)
        mixed = mixed + absorb[distance - 1] * lower + emit[distance - 1] * upper

    def sandwich(block):
        highest = lax.Precision.HIGHEST
        inner = jnp.matmul(phonon_vertex[None], block, precision=highest)
        return jnp.matmul(inner, jnp.swapaxes(phonon_vertex, -1, -2)[None], precision=highest)

    dressed = lax.map(sandwich, mixed)
    return jnp.moveaxis(dressed, 0, 1)
```

```python
import functools

import jax
import jax.numpy as jnp
from jax import lax
from jax.experimental import pallas as pl
from jax.experimental.pallas import tpu as pltpu
from jax.sharding import PartitionSpec as P

BROADENING = 1.0
LOWEST = -2.0
SPREAD = 4.0

F32 = jnp.float32
BF16 = jnp.bfloat16
VMEM_BYTES = 56 << 20


def split(x):
    high = x.astype(BF16)
    return high, (x - high.astype(F32)).astype(BF16)


def turned(x):
    half = x.shape[1] // 2
    return jnp.concatenate([-x[:, half:], x[:, :half]], axis=1)


def left_of(x):
    high, low = split(x)
    return jnp.concatenate([high, high, low], axis=1)


def right_of(x):
    high, low = split(x)
    high = jnp.concatenate([high, turned(high)], axis=0)
    low = jnp.concatenate([low, turned(low)], axis=0)
    return jnp.concatenate([high, low, high], axis=0)


def dot(a, b):
    return jnp.dot(a, b, preferred_element_type=F32)


def product(a, b):
    return dot(left_of(a), right_of(b))


def row_scaled(factor, x):
    half = x.shape[1] // 2
    real, imag = x[:, :half], x[:, half:]
    return jnp.concatenate(
        [factor[0] * real - factor[1] * imag, factor[0] * imag + factor[1] * real], axis=1
    )


def same_place(shape):
    rows = lax.broadcasted_iota(jnp.int32, shape, 0)
    cols = lax.broadcasted_iota(jnp.int32, shape, 1)
    return rows == cols


def reciprocal(real, imag):
    magnitude = real * real + imag * imag
    return real / magnitude, -imag / magnitude


def powers_of(real, imag):
    diagonal = same_place(real.shape)
    zero = jnp.zeros_like(real)
    on_real, on_imag = jnp.where(diagonal, real, zero), jnp.where(diagonal, imag, zero)
    across = reciprocal(
        jnp.sum(on_real, axis=0, keepdims=True), jnp.sum(on_imag, axis=0, keepdims=True)
    )
    down = reciprocal(
        jnp.sum(on_real, axis=1, keepdims=True), jnp.sum(on_imag, axis=1, keepdims=True)
    )
    first = jnp.concatenate(
        [
            jnp.where(diagonal, zero, imag * across[1] - real * across[0]),
            jnp.where(diagonal, zero, -(real * across[1]) - imag * across[0]),
        ],
        axis=1,
    )
    size = real.shape[0]
    second = product(first, first)
    both = dot(
        jnp.concatenate([left_of(first), left_of(second)], axis=0), right_of(second)
    )
    total = jnp.where(same_place(first.shape), 1.0, 0.0) + first + second + both[:size]
    return row_scaled(down, total), both[size:]


def energy_here():
    index = lax.axis_index("energy")
    return LOWEST + SPREAD * (index.astype(F32) + 0.5) / lax.axis_size("energy")


def upright(x):
    size = x.shape[1]
    wide = jnp.broadcast_to(x, (size, size))
    return jnp.sum(jnp.where(same_place(wide.shape), wide, jnp.zeros_like(wide)), axis=1, keepdims=True)


def bound_kernel(onsite, hopping, sigma, coupling, bound, partial, fourth, rows, term):
    size, few = hopping.shape[0], coupling.shape[1]
    diagonal = same_place(hopping.shape)
    level = energy_here() - onsite[...]
    real = jnp.where(diagonal, level, 0.0) - hopping[...] - sigma[0]
    imag = jnp.where(diagonal, BROADENING, 0.0) - sigma[1]
    scaled, power = powers_of(real, imag)
    partial[...] = scaled
    fourth[...] = power
    places = bound[...]
    pick_rows = (
        lax.broadcasted_iota(jnp.int32, (few, size), 1) == upright(places.astype(F32)).astype(jnp.int32)
    ).astype(F32).astype(BF16)
    pick_cols = (lax.broadcasted_iota(jnp.int32, (size, few), 0) == places).astype(F32).astype(BF16)
    strength = coupling[...]
    high, low = split(scaled)
    some = dot(pick_rows, high) + dot(pick_rows, low)
    some = (some + product(some, power)) * upright(strength)
    rows[...] = some
    high, low = split(jnp.concatenate([some[:, :size], some[:, size:]], axis=0))
    corner = dot(high, pick_cols) + dot(low, pick_cols)
    corner = corner * strength
    term[...] = jnp.concatenate([corner[:few], corner[few:]], axis=1)


def slab_kernel(partial, fourth, coupling, bound, inverse, columns):
    size, few = partial.shape[0], coupling.shape[1]
    whole = partial[...] + product(partial[...], fourth[...])
    inverse[...] = whole
    pick_cols = (lax.broadcasted_iota(jnp.int32, (size, few), 0) == bound[...]).astype(F32).astype(BF16)
    high, low = split(jnp.concatenate([whole[:, :size], whole[:, size:]], axis=0))
    chosen = (dot(high, pick_cols) + dot(low, pick_cols)) * coupling[...]
    columns[...] = jnp.concatenate([chosen[:size], chosen[size:]], axis=1)


def green_kernel(hamiltonian, near, far, inverse, columns, rows, green_a, green_b):
    few = hamiltonian.shape[0]
    schur = near[...] + far[...]
    diagonal = same_place(hamiltonian.shape)
    real = jnp.where(diagonal, energy_here(), 0.0) - hamiltonian[...] - schur[:, :few]
    imag = jnp.where(diagonal, BROADENING, 0.0) - schur[:, few:]
    scaled, power = powers_of(real, imag)
    separator = scaled + product(scaled, power)
    middle = product(columns[...], separator)
    green = inverse[...] + product(middle, rows[...])
    half = green_a.shape[0]
    green_a[...] = green[:half]
    green_b[...] = green[half:]


def strengths(steps, weights):
    absorb, emit = [], []
    for distance in (1, 2):
        for row, out in ((0, absorb), (1, emit)):
            total = jnp.float32(0.0)
            for mode in range(steps.shape[0]):
                total = total + jnp.where(steps[mode] == distance, weights[row, mode], 0.0)
            out.append(total)
    return absorb, emit


def combine_kernel(steps, weights, green_a, green_b, low_a, high_a, pair_b, across_a, up_b, down_b):
    absorb, emit = strengths(steps, weights)
    odd = lax.rem(lax.axis_index("energy"), 2) == 1
    zero = jnp.float32(0.0)
    own = jnp.where(odd, emit[0], absorb[0])
    lower = jnp.where(odd, absorb[0], zero)
    upper = jnp.where(odd, zero, emit[0])
    across_a[...] = own * green_a[...] + lower * low_a[...] + upper * high_a[...]
    up_b[...] = absorb[1] * green_b[...] + jnp.where(odd, zero, absorb[0]) * pair_b[...]
    down_b[...] = emit[1] * green_b[...] + jnp.where(odd, emit[0], zero) * pair_b[...]


def dress_kernel(steps, weights, vertex, low_a, high_a, across_a, up_b, down_b, pair_b, out):
    absorb, emit = strengths(steps, weights)
    odd = lax.rem(lax.axis_index("energy"), 2) == 1
    mixed_a = absorb[1] * low_a[...] + emit[1] * high_a[...] + across_a[...]
    mixed_b = up_b[...] + down_b[...] + jnp.where(odd, absorb[0], emit[0]) * pair_b[...]
    mixed = jnp.concatenate([mixed_a, mixed_b], axis=0)
    size = vertex.shape[0]
    high, low = split(mixed)
    vertex_high, vertex_low = split(vertex[...])
    inner = dot(
        jnp.concatenate([vertex_high, vertex_high, vertex_low], axis=1),
        jnp.concatenate([high, low, high], axis=0),
    )
    inner = jnp.concatenate([inner[:, :size], inner[:, size:]], axis=0)
    high, low = split(inner)
    flipped = vertex[...].T
    flipped_high, flipped_low = split(flipped)
    outer = dot(
        jnp.concatenate([high, high, low], axis=1),
        jnp.concatenate([flipped_high, flipped_low, flipped_high], axis=0),
    )
    out[0] = outer[:size]
    out[1] = outer[size:]


def call(kernel, outs, args, scalars=0, flops=0):
    vmem = pl.BlockSpec(memory_space=pltpu.VMEM)
    smem = pl.BlockSpec(memory_space=pltpu.SMEM)
    touched = sum(4 * a.size for a in [*args, *jax.tree.leaves(outs)])
    return pl.pallas_call(
        kernel,
        out_shape=outs,
        in_specs=[smem] * scalars + [vmem] * (len(args) - scalars),
        out_specs=jax.tree.map(lambda _: vmem, outs),
        compiler_params=pltpu.CompilerParams(vmem_limit_bytes=VMEM_BYTES),
        cost_estimate=pl.CostEstimate(flops=flops, bytes_accessed=touched, transcendentals=0),
    )(*args)


def held(*shape):
    return jax.ShapeDtypeStruct(shape, F32)


def moved(x, axis, pairs):
    return lax.ppermute(x, axis, pairs)


def per_device(
    onsite,
    hopping,
    separator_hamiltonian,
    coupling,
    bound_rows,
    old_sigma,
    phonon_vertex,
    mode_steps,
    mode_weights,
):
    size, few = hopping.shape[-1], coupling.shape[-1]
    energies, slabs = lax.axis_size("energy"), lax.axis_size("slab")
    assert energies % 2 == 0 and slabs & (slabs - 1) == 0
    half = size // 2
    cube = 3 * 8 * size**3
    sigma = old_sigma.reshape(2, size, size)
    partial, fourth, rows, term = call(
        bound_kernel,
        [held(size, 2 * size), held(size, 2 * size), held(few, 2 * size), held(few, 2 * few)],
        [onsite, hopping[0], sigma, coupling, bound_rows],
        flops=4 * cube,
    )
    near, far = None, term
    reach = 1
    while reach < slabs:
        near = far if near is None else near + far
        far = moved(near, "slab", [(i, i ^ reach) for i in range(slabs)])
        reach *= 2
    inverse, columns = call(
        slab_kernel,
        [held(size, 2 * size), held(size, 2 * few)],
        [partial, fourth, coupling, bound_rows],
        flops=cube,
    )
    green_a, green_b = call(
        green_kernel,
        [held(half, 2 * size), held(half, 2 * size)],
        [separator_hamiltonian, near, far, inverse, columns, rows],
        flops=cube,
    )
    upward = [(i, i + 2) for i in range(energies - 2)]
    downward = [(i + 2, i) for i in range(energies - 2)]
    pairwise = [(i, i ^ 1) for i in range(energies)]
    low_a = moved(green_a, "energy", upward)
    high_a = moved(green_a, "energy", downward)
    pair_b = moved(green_b, "energy", pairwise)
    across_a, up_b, down_b = call(
        combine_kernel,
        [held(half, 2 * size)] * 3,
        [mode_steps, mode_weights, green_a, green_b, low_a, high_a, pair_b],
        scalars=2,
    )
    across_a = moved(across_a, "energy", pairwise)
    up_b = moved(up_b, "energy", upward)
    down_b = moved(down_b, "energy", downward)
    out = call(
        dress_kernel,
        held(2, size, size),
        [mode_steps, mode_weights, phonon_vertex[0], low_a, high_a, across_a, up_b, down_b, pair_b],
        scalars=2,
        flops=cube,
    )
    return out.reshape(old_sigma.shape)


def solution(mesh):
    placed = (
        P("slab", None),
        P("slab", None, None),
        P(),
        P("slab", None),
        P("slab", None),
        P(None, "energy", "slab", None, None),
        P("slab", None, None),
        P(),
        P(),
    )
    return jax.shard_map(
        per_device,
        mesh=mesh,
        in_specs=placed,
        out_specs=P(None, "energy", "slab", None, None),
        check_vma=False,
    )
```

```python
import functools

import jax
import jax.numpy as jnp
from jax import lax
from jax.experimental import pallas as pl
from jax.experimental.pallas import tpu as pltpu
from jax.sharding import PartitionSpec as P

BROADENING = 1.0
LOWEST = -2.0
SPREAD = 4.0

F32 = jnp.float32
BF16 = jnp.bfloat16
VMEM_BYTES = 24 << 20


def split(x):
    high = x.astype(BF16)
    return high, (x - high.astype(F32)).astype(BF16)


def turned(x):
    half = x.shape[1] // 2
    return jnp.concatenate([-x[:, half:], x[:, :half]], axis=1)


def left_of(x):
    high, low = split(x)
    return jnp.concatenate([high, high, low], axis=1)


def right_of(x):
    high, low = split(x)
    high = jnp.concatenate([high, turned(high)], axis=0)
    low = jnp.concatenate([low, turned(low)], axis=0)
    return jnp.concatenate([high, low, high], axis=0)


def dot(a, b):
    return jnp.dot(a, b, preferred_element_type=F32)


def product(a, b):
    return dot(left_of(a), right_of(b))


def row_scaled(factor, x):
    half = x.shape[1] // 2
    real, imag = x[:, :half], x[:, half:]
    return jnp.concatenate(
        [factor[0] * real - factor[1] * imag, factor[0] * imag + factor[1] * real], axis=1
    )


def same_place(shape):
    rows = lax.broadcasted_iota(jnp.int32, shape, 0)
    cols = lax.broadcasted_iota(jnp.int32, shape, 1)
    return rows == cols


def reciprocal(real, imag):
    magnitude = real * real + imag * imag
    return real / magnitude, -imag / magnitude


def reciprocal_diagonal(real, imag):
    tile = 128
    ways = ([], [])
    for at in range(0, real.shape[0], tile):
        blocks = [x[at : at + tile, at : at + tile] for x in (real, imag)]
        diagonal = same_place(blocks[0].shape)
        blocks = [jnp.where(diagonal, x, jnp.zeros_like(x)) for x in blocks]
        for axis in (0, 1):
            ways[axis].append([jnp.sum(x, axis=axis, keepdims=True) for x in blocks])
    across = [jnp.concatenate(part, axis=1) for part in zip(*ways[0])]
    down = [jnp.concatenate(part, axis=0) for part in zip(*ways[1])]
    return reciprocal(*across), reciprocal(*down)


def remainder(real, imag, across):
    diagonal = same_place(real.shape)
    zero = jnp.zeros_like(real)
    return jnp.concatenate(
        [
            jnp.where(diagonal, zero, imag * across[1] - real * across[0]),
            jnp.where(diagonal, zero, -(real * across[1]) - imag * across[0]),
        ],
        axis=1,
    )


def unit(shape):
    return jnp.where(same_place(shape), 1.0, 0.0)


def energy_here():
    index = lax.axis_index("energy")
    return LOWEST + SPREAD * (index.astype(F32) + 0.5) / lax.axis_size("energy")


def upright(x):
    size = x.shape[1]
    wide = jnp.broadcast_to(x, (size, size))
    return jnp.sum(jnp.where(same_place(wide.shape), wide, jnp.zeros_like(wide)), axis=1, keepdims=True)


def bound_kernel(onsite, hopping, sigma, coupling, bound, first_out, second_out, start_out, rows, term):
    size, few = hopping.shape[0], coupling.shape[1]
    diagonal = same_place(hopping.shape)
    level = energy_here() - onsite[...]
    real = jnp.where(diagonal, level, 0.0) - hopping[...] - sigma[0]
    imag = jnp.where(diagonal, BROADENING, 0.0) - sigma[1]
    across, down = reciprocal_diagonal(real, imag)
    first = remainder(real, imag, across)
    first_out[...] = first
    start_out[...] = jnp.concatenate(down, axis=1)
    second = product(first, first)
    second_out[...] = second
    places = bound[...]
    pick_rows = (
        lax.broadcasted_iota(jnp.int32, (few, size), 1) == upright(places.astype(F32)).astype(jnp.int32)
    ).astype(F32).astype(BF16)
    pick_cols = (lax.broadcasted_iota(jnp.int32, (size, few), 0) == places).astype(F32).astype(BF16)
    strength = coupling[...]
    high, low = split(row_scaled(down, unit(first.shape) + first))
    some = dot(pick_rows, high) + dot(pick_rows, low)
    right = right_of(second)
    some = some + dot(left_of(some), right)
    some = some + dot(left_of(dot(left_of(some), right)), right)
    some = some * upright(strength)
    rows[...] = some
    high, low = split(jnp.concatenate([some[:, :size], some[:, size:]], axis=0))
    corner = dot(high, pick_cols) + dot(low, pick_cols)
    corner = corner * strength
    term[...] = jnp.concatenate([corner[:few], corner[few:]], axis=1)


def power_kernel(first, second, start, partial, fourth):
    size = first.shape[0]
    one, two = first[...], second[...]
    both = dot(jnp.concatenate([left_of(one), left_of(two)], axis=0), right_of(two))
    total = unit(one.shape) + one + two + both[:size]
    partial[...] = row_scaled((start[:, 0:1], start[:, 1:2]), total)
    fourth[...] = both[size:]


def slab_kernel(partial, fourth, coupling, bound, inverse, columns):
    size, few = partial.shape[0], coupling.shape[1]
    whole = partial[...] + product(partial[...], fourth[...])
    inverse[...] = whole
    pick_cols = (lax.broadcasted_iota(jnp.int32, (size, few), 0) == bound[...]).astype(F32).astype(BF16)
    high, low = split(jnp.concatenate([whole[:, :size], whole[:, size:]], axis=0))
    chosen = (dot(high, pick_cols) + dot(low, pick_cols)) * coupling[...]
    columns[...] = jnp.concatenate([chosen[:size], chosen[size:]], axis=1)


def green_kernel(hamiltonian, inverse, columns, rows, *terms_and_greens):
    terms, (green_a, green_b) = terms_and_greens[:-2], terms_and_greens[-2:]
    few = hamiltonian.shape[0]
    schur = terms[0][...]
    for term in terms[1:]:
        schur = schur + term[...]
    diagonal = same_place(hamiltonian.shape)
    real = jnp.where(diagonal, energy_here(), 0.0) - hamiltonian[...] - schur[:, :few]
    imag = jnp.where(diagonal, BROADENING, 0.0) - schur[:, few:]
    across, down = reciprocal_diagonal(real, imag)
    first = remainder(real, imag, across)
    second = product(first, first)
    both = dot(jnp.concatenate([left_of(first), left_of(second)], axis=0), right_of(second))
    total = row_scaled(down, unit(first.shape) + first + second + both[:few])
    separator = total + product(total, both[few:])
    middle = product(columns[...], separator)
    green = inverse[...] + product(middle, rows[...])
    half = green_a.shape[0]
    green_a[...] = green[:half]
    green_b[...] = green[half:]


def strengths(steps, weights):
    absorb, emit = [], []
    for distance in (1, 2):
        for row, out in ((0, absorb), (1, emit)):
            total = jnp.float32(0.0)
            for mode in range(steps.shape[0]):
                total = total + jnp.where(steps[mode] == distance, weights[row, mode], 0.0)
            out.append(total)
    return absorb, emit


def place():
    energy, count = lax.axis_index("energy"), lax.axis_size("energy")
    odd = lax.rem(energy, 2) == 1
    odd_pair = lax.rem(lax.div(energy, 2), 2) == 1
    lower, higher = energy >= 2, energy + 2 < count
    one = jnp.where(odd_pair, lower.astype(jnp.int32), higher.astype(jnp.int32)) == 1
    two = jnp.where(odd_pair, higher.astype(jnp.int32), lower.astype(jnp.int32)) == 1
    return odd, odd_pair, one, two


def kept(there, x):
    return jnp.where(there, x, jnp.zeros_like(x))


def combine_kernel(steps, weights, green_a, green_b, one_a, two_a, pair_b, across_a, one_b, two_b):
    absorb, emit = strengths(steps, weights)
    odd, odd_pair, one, two = place()
    zero = jnp.float32(0.0)
    from_one = jnp.where(odd, jnp.where(odd_pair, absorb[0], zero), jnp.where(odd_pair, zero, emit[0]))
    from_two = jnp.where(odd, jnp.where(odd_pair, zero, absorb[0]), jnp.where(odd_pair, emit[0], zero))
    across_a[...] = (
        jnp.where(odd, emit[0], absorb[0]) * green_a[...]
        + from_one * kept(one, one_a[...])
        + from_two * kept(two, two_a[...])
    )
    up = (absorb[1], jnp.where(odd, zero, absorb[0]))
    down = (emit[1], jnp.where(odd, emit[0], zero))
    for out, first, second in ((one_b, up, down), (two_b, down, up)):
        own, other = [jnp.where(odd_pair, b, a) for a, b in zip(first, second)]
        out[...] = own * green_b[...] + other * pair_b[...]


def dress_kernel(steps, weights, vertex, one_a, two_a, across_a, one_b, two_b, pair_b, out):
    absorb, emit = strengths(steps, weights)
    odd, odd_pair, one, two = place()
    from_one = jnp.where(odd_pair, absorb[1], emit[1])
    from_two = jnp.where(odd_pair, emit[1], absorb[1])
    mixed_a = from_one * kept(one, one_a[...]) + from_two * kept(two, two_a[...]) + across_a[...]
    mixed_b = (
        kept(one, one_b[...]) + kept(two, two_b[...]) + jnp.where(odd, absorb[0], emit[0]) * pair_b[...]
    )
    mixed = jnp.concatenate([mixed_a, mixed_b], axis=0)
    size = vertex.shape[0]
    high, low = split(mixed)
    vertex_high, vertex_low = split(vertex[...])
    inner = dot(
        jnp.concatenate([vertex_high, vertex_high, vertex_low], axis=1),
        jnp.concatenate([high, low, high], axis=0),
    )
    inner = jnp.concatenate([inner[:, :size], inner[:, size:]], axis=0)
    high, low = split(inner)
    flipped = vertex[...].T
    flipped_high, flipped_low = split(flipped)
    outer = dot(
        jnp.concatenate([high, high, low], axis=1),
        jnp.concatenate([flipped_high, flipped_low, flipped_high], axis=0),
    )
    out[0] = outer[:size]
    out[1] = outer[size:]


def call(kernel, outs, args, scalars=0, flops=0):
    vmem = pl.BlockSpec(memory_space=pltpu.VMEM)
    smem = pl.BlockSpec(memory_space=pltpu.SMEM)
    touched = sum(4 * a.size for a in [*args, *jax.tree.leaves(outs)])
    return pl.pallas_call(
        kernel,
        out_shape=outs,
        in_specs=[smem] * scalars + [vmem] * (len(args) - scalars),
        out_specs=jax.tree.map(lambda _: vmem, outs),
        compiler_params=pltpu.CompilerParams(vmem_limit_bytes=VMEM_BYTES),
        cost_estimate=pl.CostEstimate(flops=flops, bytes_accessed=touched, transcendentals=0),
    )(*args)


def held(*shape):
    return jax.ShapeDtypeStruct(shape, F32)


def exchange(x, partner):
    slabs, energies = lax.axis_size("slab"), lax.axis_size("energy")
    pairs = []
    for slab in range(slabs):
        for energy in range(energies):
            other = partner(energy)
            if 0 <= other < energies:
                target = slab * energies + other
            else:
                target = (slab ^ 1) % slabs * energies + energy
            pairs.append((slab * energies + energy, target))
    return lax.ppermute(x, ("slab", "energy"), pairs)


def in_pair(energy):
    return energy ^ 1


def in_one(energy):
    return energy ^ 2


def in_two(energy):
    return energy + 2 if energy // 2 % 2 == 1 else energy - 2


def per_device(
    onsite,
    hopping,
    separator_hamiltonian,
    coupling,
    bound_rows,
    old_sigma,
    phonon_vertex,
    mode_steps,
    mode_weights,
):
    size, few = hopping.shape[-1], coupling.shape[-1]
    energies, slabs = lax.axis_size("energy"), lax.axis_size("slab")
    assert energies % 2 == 0 and slabs & (slabs - 1) == 0
    half = size // 2
    cube = 3 * 8 * size**3
    full = held(size, 2 * size)
    sigma = old_sigma.reshape(2, size, size)
    first, second, start, rows, term = call(
        bound_kernel,
        [full, full, held(size, 2), held(few, 2 * size), held(few, 2 * few)],
        [onsite, hopping[0], sigma, coupling, bound_rows],
        flops=2 * cube,
    )
    partial, fourth = call(power_kernel, [full, full], [first, second, start], flops=2 * cube)
    terms, ahead = [term], []
    reach = slabs // 2
    while reach:
        swap = [(i, i ^ reach) for i in range(slabs)]
        if ahead:
            *ahead, fourth = lax.optimization_barrier((*ahead, fourth))
            terms = [term, *ahead]
        ahead = ahead + [lax.ppermute(x, "slab", swap) for x in terms]
        terms = [term, *ahead]
        reach //= 2
    inverse, columns = call(
        slab_kernel,
        [full, held(size, 2 * few)],
        [partial, fourth, coupling, bound_rows],
        flops=cube,
    )
    green_a, green_b = call(
        green_kernel,
        [held(half, 2 * size), held(half, 2 * size)],
        [separator_hamiltonian, inverse, columns, rows, *terms],
        flops=cube,
    )
    two_a = exchange(green_a, in_two)
    one_a = exchange(green_a, in_one)
    pair_b = exchange(green_b, in_pair)
    across_a, one_b, two_b = call(
        combine_kernel,
        [held(half, 2 * size)] * 3,
        [mode_steps, mode_weights, green_a, green_b, one_a, two_a, pair_b],
        scalars=2,
    )
    two_b = exchange(two_b, in_two)
    one_b = exchange(one_b, in_one)
    across_a = exchange(across_a, in_pair)
    out = call(
        dress_kernel,
        held(2, size, size),
        [mode_steps, mode_weights, phonon_vertex[0], one_a, two_a, across_a, one_b, two_b, pair_b],
        scalars=2,
        flops=cube,
    )
    return out.reshape(old_sigma.shape)


def solution(mesh):
    placed = (
        P("slab", None),
        P("slab", None, None),
        P(),
        P("slab", None),
        P("slab", None),
        P(None, "energy", "slab", None, None),
        P("slab", None, None),
        P(),
        P(),
    )
    return jax.shard_map(
        per_device,
        mesh=mesh,
        in_specs=placed,
        out_specs=P(None, "energy", "slab", None, None),
        check_vma=False,
    )
```

```python
import functools

import jax
import jax.numpy as jnp
from jax import lax
from jax.experimental import pallas as pl
from jax.experimental.pallas import tpu as pltpu
from jax.sharding import PartitionSpec as P

BROADENING = 1.0
LOWEST = -2.0
SPREAD = 4.0

F32 = jnp.float32
BF16 = jnp.bfloat16
VMEM_BYTES = 24 << 20


def split(x):
    high = x.astype(BF16)
    return high, (x - high.astype(F32)).astype(BF16)


def turned(x):
    half = x.shape[1] // 2
    return jnp.concatenate([-x[:, half:], x[:, :half]], axis=1)


def left_of(x):
    high, low = split(x)
    return jnp.concatenate([high, high, low], axis=1)


def right_of(x):
    high, low = split(x)
    high = jnp.concatenate([high, turned(high)], axis=0)
    low = jnp.concatenate([low, turned(low)], axis=0)
    return jnp.concatenate([high, low, high], axis=0)


def dot(a, b):
    return jnp.dot(a, b, preferred_element_type=F32)


def product(a, b):
    return dot(left_of(a), right_of(b))


def row_scaled(factor, x):
    half = x.shape[1] // 2
    real, imag = x[:, :half], x[:, half:]
    return jnp.concatenate(
        [factor[0] * real - factor[1] * imag, factor[0] * imag + factor[1] * real], axis=1
    )


def same_place(shape):
    rows = lax.broadcasted_iota(jnp.int32, shape, 0)
    cols = lax.broadcasted_iota(jnp.int32, shape, 1)
    return rows == cols


def reciprocal(real, imag):
    magnitude = real * real + imag * imag
    return real / magnitude, -imag / magnitude


def reciprocal_diagonal(real, imag):
    tile = 128
    ways = ([], [])
    for at in range(0, real.shape[0], tile):
        blocks = [x[at : at + tile, at : at + tile] for x in (real, imag)]
        diagonal = same_place(blocks[0].shape)
        blocks = [jnp.where(diagonal, x, jnp.zeros_like(x)) for x in blocks]
        for axis in (0, 1):
            ways[axis].append([jnp.sum(x, axis=axis, keepdims=True) for x in blocks])
    across = [jnp.concatenate(part, axis=1) for part in zip(*ways[0])]
    down = [jnp.concatenate(part, axis=0) for part in zip(*ways[1])]
    return reciprocal(*across), reciprocal(*down)


def remainder(real, imag, across):
    diagonal = same_place(real.shape)
    zero = jnp.zeros_like(real)
    return jnp.concatenate(
        [
            jnp.where(diagonal, zero, imag * across[1] - real * across[0]),
            jnp.where(diagonal, zero, -(real * across[1]) - imag * across[0]),
        ],
        axis=1,
    )


def unit(shape):
    return jnp.where(same_place(shape), 1.0, 0.0)


def energy_here():
    index = lax.axis_index("energy")
    return LOWEST + SPREAD * (index.astype(F32) + 0.5) / lax.axis_size("energy")


def upright(x):
    size = x.shape[1]
    wide = jnp.broadcast_to(x, (size, size))
    return jnp.sum(jnp.where(same_place(wide.shape), wide, jnp.zeros_like(wide)), axis=1, keepdims=True)


def bound_kernel(*refs):
    sources, outs = refs[:5], refs[5:10]
    onsite, hopping, sigma, coupling, bound = places = refs[10:15]
    first_out, second_out, start_out, rows, term = outs
    arrived = refs[15]
    copies = [
        pltpu.make_async_copy(source, target, arrived.at[at])
        for at, (source, target) in enumerate(zip(sources, places))
    ]
    for copy in copies:
        copy.start()
    for copy in copies:
        copy.wait()
    size, few = hopping.shape[0], coupling.shape[1]
    diagonal = same_place(hopping.shape)
    level = energy_here() - onsite[...]
    real = jnp.where(diagonal, level, 0.0) - hopping[...] - sigma[0]
    imag = jnp.where(diagonal, BROADENING, 0.0) - sigma[1]
    across, down = reciprocal_diagonal(real, imag)
    first = remainder(real, imag, across)
    first_out[...] = first
    start_out[...] = jnp.concatenate(down, axis=1)
    second = product(first, first)
    second_out[...] = second
    places = bound[...]
    pick_rows = (
        lax.broadcasted_iota(jnp.int32, (few, size), 1) == upright(places.astype(F32)).astype(jnp.int32)
    ).astype(F32).astype(BF16)
    pick_cols = (lax.broadcasted_iota(jnp.int32, (size, few), 0) == places).astype(F32).astype(BF16)
    strength = coupling[...]
    high, low = split(row_scaled(down, unit(first.shape) + first))
    some = dot(pick_rows, high) + dot(pick_rows, low)
    right = right_of(second)
    some = some + dot(left_of(some), right)
    some = some + dot(left_of(dot(left_of(some), right)), right)
    some = some * upright(strength)
    rows[...] = some
    high, low = split(jnp.concatenate([some[:, :size], some[:, size:]], axis=0))
    corner = dot(high, pick_cols) + dot(low, pick_cols)
    corner = corner * strength
    term[...] = jnp.concatenate([corner[:few], corner[few:]], axis=1)


def slab_kernel(first, second, start, inverse):
    size = first.shape[0]
    one, two = first[...], second[...]
    both = dot(jnp.concatenate([left_of(one), left_of(two)], axis=0), right_of(two))
    total = row_scaled((start[:, 0:1], start[:, 1:2]), unit(one.shape) + one + two + both[:size])
    inverse[...] = total + product(total, both[size:])


def column_kernel(inverse, coupling, bound, columns):
    size, few = inverse.shape[0], coupling.shape[1]
    whole = inverse[...]
    pick_cols = (lax.broadcasted_iota(jnp.int32, (size, few), 0) == bound[...]).astype(F32).astype(BF16)
    high, low = split(jnp.concatenate([whole[:, :size], whole[:, size:]], axis=0))
    chosen = (dot(high, pick_cols) + dot(low, pick_cols)) * coupling[...]
    columns[...] = jnp.concatenate([chosen[:size], chosen[size:]], axis=1)


def green_kernel(hamiltonian, inverse, columns, rows, near, far, *greens):
    few = hamiltonian.shape[0]
    schur = near[...] + far[...]
    diagonal = same_place(hamiltonian.shape)
    real = jnp.where(diagonal, energy_here(), 0.0) - hamiltonian[...] - schur[:, :few]
    imag = jnp.where(diagonal, BROADENING, 0.0) - schur[:, few:]
    across, down = reciprocal_diagonal(real, imag)
    first = remainder(real, imag, across)
    second = product(first, first)
    both = dot(jnp.concatenate([left_of(first), left_of(second)], axis=0), right_of(second))
    total = row_scaled(down, unit(first.shape) + first + second + both[:few])
    separator = total + product(total, both[few:])
    middle = product(columns[...], separator)
    green = inverse[...] + product(middle, rows[...])
    half, size = greens[0].shape
    for at, part in enumerate((green[:, :size], green[:, size:])):
        greens[2 * at][...] = part[:half]
        greens[2 * at + 1][...] = part[half:]


def strengths(steps, weights):
    absorb, emit = [], []
    for distance in (1, 2):
        for row, out in ((0, absorb), (1, emit)):
            total = jnp.float32(0.0)
            for mode in range(steps.shape[0]):
                total = total + jnp.where(steps[mode] == distance, weights[row, mode], 0.0)
            out.append(total)
    return absorb, emit


def place():
    energy, count = lax.axis_index("energy"), lax.axis_size("energy")
    odd = lax.rem(energy, 2) == 1
    odd_pair = lax.rem(lax.div(energy, 2), 2) == 1
    lower, higher = energy >= 2, energy + 2 < count
    one = jnp.where(odd_pair, lower.astype(jnp.int32), higher.astype(jnp.int32)) == 1
    two = jnp.where(odd_pair, higher.astype(jnp.int32), lower.astype(jnp.int32)) == 1
    return odd, odd_pair, one, two


def kept(there, x):
    return jnp.where(there, x, jnp.zeros_like(x))


def combine_kernel(steps, weights, green_a, green_b, one_a, two_a, pair_b, across_a, one_b, two_b):
    absorb, emit = strengths(steps, weights)
    odd, odd_pair, one, two = place()
    zero = jnp.float32(0.0)
    from_one = jnp.where(odd, jnp.where(odd_pair, absorb[0], zero), jnp.where(odd_pair, zero, emit[0]))
    from_two = jnp.where(odd, jnp.where(odd_pair, zero, absorb[0]), jnp.where(odd_pair, emit[0], zero))
    across_a[...] = (
        jnp.where(odd, emit[0], absorb[0]) * green_a[...]
        + from_one * kept(one, one_a[...])
        + from_two * kept(two, two_a[...])
    )
    up = (absorb[1], jnp.where(odd, zero, absorb[0]))
    down = (emit[1], jnp.where(odd, emit[0], zero))
    for out, first, second in ((one_b, up, down), (two_b, down, up)):
        own, other = [jnp.where(odd_pair, b, a) for a, b in zip(first, second)]
        out[...] = own * green_b[...] + other * pair_b[...]


def dress_kernel(steps, weights, vertex_left, vertex_right, one_a, two_a, across_a, one_b, two_b, pair_b, *rest):
    out = rest[-1]
    absorb, emit = strengths(steps, weights)
    odd, odd_pair, one, two = place()
    from_one = jnp.where(odd_pair, absorb[1], emit[1])
    from_two = jnp.where(odd_pair, emit[1], absorb[1])
    mixed_a = from_one * kept(one, one_a[...]) + from_two * kept(two, two_a[...]) + across_a[...]
    mixed_b = (
        kept(one, one_b[...]) + kept(two, two_b[...]) + jnp.where(odd, absorb[0], emit[0]) * pair_b[...]
    )
    mixed = jnp.concatenate([mixed_a, mixed_b], axis=0)
    high, low = split(mixed)
    inner = dot(vertex_left[...], jnp.concatenate([high, low, high], axis=0))
    high, low = split(inner)
    out[0] = dot(jnp.concatenate([high, high, low], axis=1), vertex_right[...])


def vertex_kernel(vertex, left, right):
    size = vertex.shape[0]
    high, low = split(vertex[...])
    for at, part in enumerate((high, high, low)):
        left[:, at * size : (at + 1) * size] = part
    high, low = split(vertex[...].T)
    for at, part in enumerate((high, low, high)):
        right[at * size : (at + 1) * size, :] = part


def call(kernel, outs, args, scalars=0, flops=0, **kept):
    vmem = pl.BlockSpec(memory_space=pltpu.VMEM)
    smem = pl.BlockSpec(memory_space=pltpu.SMEM)
    touched = sum(4 * a.size for a in [*args, *jax.tree.leaves(outs)])
    settings = dict(
        in_specs=[smem] * scalars + [vmem] * (len(args) - scalars),
        out_specs=jax.tree.map(lambda _: vmem, outs),
    )
    settings.update(kept)
    return pl.pallas_call(
        kernel,
        out_shape=outs,
        compiler_params=pltpu.CompilerParams(vmem_limit_bytes=VMEM_BYTES),
        cost_estimate=pl.CostEstimate(flops=flops, bytes_accessed=touched, transcendentals=0),
        **settings,
    )(*args)


def held(*shape):
    return jax.ShapeDtypeStruct(shape, F32)


def exchange(x, partner):
    slabs, energies = lax.axis_size("slab"), lax.axis_size("energy")
    pairs = []
    for slab in range(slabs):
        for energy in range(energies):
            other = partner(energy)
            if 0 <= other < energies:
                target = slab * energies + other
            else:
                target = (slab ^ 1) % slabs * energies + energy
            pairs.append((slab * energies + energy, target))
    return lax.ppermute(x, ("slab", "energy"), pairs)


def in_pair(energy):
    return energy ^ 1


def in_one(energy):
    return energy ^ 2


def in_two(energy):
    return energy + 2 if energy // 2 % 2 == 1 else energy - 2


def per_device(
    onsite,
    hopping,
    separator_hamiltonian,
    coupling,
    bound_rows,
    old_sigma,
    phonon_vertex,
    mode_steps,
    mode_weights,
):
    size, few = hopping.shape[-1], coupling.shape[-1]
    energies, slabs = lax.axis_size("energy"), lax.axis_size("slab")
    assert energies % 2 == 0 and slabs & (slabs - 1) == 0
    half = size // 2
    cube = 3 * 8 * size**3
    full = held(size, 2 * size)
    sigma = old_sigma.reshape(2, size, size)
    given = [
        pltpu.with_memory_space_constraint(x, pltpu.HBM)
        for x in (onsite, hopping[0], sigma, coupling, bound_rows)
    ]
    first, second, start, rows, term = call(
        bound_kernel,
        [full, full, held(size, 2), held(few, 2 * size), held(few, 2 * few)],
        given,
        flops=2 * cube,
        in_specs=[pl.BlockSpec(memory_space=pltpu.HBM)] * len(given),
        scratch_shapes=[pltpu.VMEM(x.shape, x.dtype) for x in given]
        + [pltpu.SemaphoreType.DMA((len(given),))],
    )
    inverse = call(slab_kernel, full, [first, second, start], flops=3 * cube)
    near, far, reach = term, None, slabs // 2
    while reach:
        if far is not None:
            far, inverse = lax.optimization_barrier((far, inverse))
            near = near + far
        far = lax.ppermute(near, "slab", [(i, i ^ reach) for i in range(slabs)])
        reach //= 2
    columns = call(column_kernel, held(size, 2 * few), [inverse, coupling, bound_rows], flops=cube // 8)
    greens = call(
        green_kernel,
        [held(half, size)] * 4,
        [separator_hamiltonian, inverse, columns, rows, near, far],
        flops=cube,
    )
    parts = []
    for green_a, green_b in (greens[:2], greens[2:]):
        two_a = exchange(green_a, in_two)
        one_a = exchange(green_a, in_one)
        pair_b = exchange(green_b, in_pair)
        parts.append((green_a, green_b, one_a, two_a, pair_b))
    combined = []
    for part in parts:
        across_a, one_b, two_b = call(
            combine_kernel,
            [held(half, size)] * 3,
            [mode_steps, mode_weights, *part],
            scalars=2,
        )
        two_b = exchange(two_b, in_two)
        one_b = exchange(one_b, in_one)
        across_a = exchange(across_a, in_pair)
        combined.append((across_a, one_b, two_b))
    vertex = call(
        vertex_kernel,
        [jax.ShapeDtypeStruct((size, 3 * size), BF16), jax.ShapeDtypeStruct((3 * size, size), BF16)],
        [phonon_vertex[0]],
    )
    out = None
    for at, (part, more) in enumerate(zip(parts, combined)):
        args = [mode_steps, mode_weights, *vertex, part[2], part[3], *more, part[4]]
        vmem = pl.BlockSpec(memory_space=pltpu.VMEM)
        specs = [pl.BlockSpec(memory_space=pltpu.SMEM)] * 2 + [vmem] * (len(args) - 2)
        aliases = {}
        if out is not None:
            aliases = {len(args): 0}
            args, specs = [*args, out], [*specs, pl.BlockSpec(memory_space=pl.ANY)]
        out = call(
            dress_kernel,
            held(2, size, size),
            args,
            flops=cube // 4,
            in_specs=specs,
            grid=(1,),
            out_specs=pl.BlockSpec((1, size, size), functools.partial(lambda at, i: (at, 0, 0), at)),
            input_output_aliases=aliases,
        )
    return out.reshape(old_sigma.shape)


def solution(mesh):
    placed = (
        P("slab", None),
        P("slab", None, None),
        P(),
        P("slab", None),
        P("slab", None),
        P(None, "energy", "slab", None, None),
        P("slab", None, None),
        P(),
        P(),
    )
    return jax.shard_map(
        per_device,
        mesh=mesh,
        in_specs=placed,
        out_specs=P(None, "energy", "slab", None, None),
        check_vma=False,
    )
```

```python
import functools

import jax
import jax.numpy as jnp
from jax import lax
from jax.experimental import pallas as pl
from jax.experimental.pallas import tpu as pltpu
from jax.sharding import PartitionSpec as P

BROADENING = 1.0
LOWEST = -2.0
SPREAD = 4.0

F32 = jnp.float32
BF16 = jnp.bfloat16
VMEM_BYTES = 24 << 20


def split(x):
    high = x.astype(BF16)
    return high, (x - high.astype(F32)).astype(BF16)


def turned(x):
    half = x.shape[1] // 2
    return jnp.concatenate([-x[:, half:], x[:, :half]], axis=1)


def left_of(x):
    high, low = split(x)
    return jnp.concatenate([high, high, low], axis=1)


def right_of(x):
    high, low = split(x)
    high = jnp.concatenate([high, turned(high)], axis=0)
    low = jnp.concatenate([low, turned(low)], axis=0)
    return jnp.concatenate([high, low, high], axis=0)


def dot(a, b):
    return jnp.dot(a, b, preferred_element_type=F32)


def product(a, b):
    return dot(left_of(a), right_of(b))


def column_scaled(x, factor):
    half = x.shape[1] // 2
    real, imag = x[:, :half], x[:, half:]
    return jnp.concatenate(
        [real * factor[0] - imag * factor[1], imag * factor[0] + real * factor[1]], axis=1
    )


def stacked(x):
    half = x.shape[1] // 2
    return jnp.concatenate([x[:, :half], x[:, half:]], axis=0)


def beside(x):
    half = x.shape[0] // 2
    return jnp.concatenate([x[:half], x[half:]], axis=1)


def columns_of(high, low, places):
    rows = lax.broadcasted_iota(jnp.int32, (high.shape[0], places.shape[1]), 0)
    pick = (rows == places).astype(F32).astype(BF16)
    return beside(dot(stacked(high), pick) + dot(stacked(low), pick))


def rows_of(high, low, places):
    shape = (places.shape[1], high.shape[0])
    pick = lax.broadcasted_iota(jnp.int32, shape, 1) == upright(places.astype(F32)).astype(jnp.int32)
    pick = pick.astype(F32).astype(BF16)
    return dot(pick, high) + dot(pick, low)


def twice(row):
    return jnp.concatenate([row, row], axis=1)


def same_place(shape):
    rows = lax.broadcasted_iota(jnp.int32, shape, 0)
    cols = lax.broadcasted_iota(jnp.int32, shape, 1)
    return rows == cols


def reciprocal(real, imag):
    magnitude = real * real + imag * imag
    return real / magnitude, -imag / magnitude


TILE = 128


def start_of(real, imag, row):
    count = real.shape[0]
    blocks = [x[:, row : row + count] for x in (real, imag)]
    diagonal = same_place(blocks[0].shape)
    blocks = [jnp.where(diagonal, x, jnp.zeros_like(x)) for x in blocks]
    return [
        reciprocal(*[jnp.sum(x, axis=axis, keepdims=True) for x in blocks]) for axis in (1, 0)
    ]


def remainder(real, imag, down, row):
    rows = lax.broadcasted_iota(jnp.int32, real.shape, 0) + row
    off = rows != lax.broadcasted_iota(jnp.int32, real.shape, 1)
    zero = jnp.zeros_like(real)
    return jnp.concatenate(
        [
            jnp.where(off, down[1] * imag - down[0] * real, zero),
            jnp.where(off, -(down[1] * real) - down[0] * imag, zero),
        ],
        axis=1,
    )


def unit(shape):
    return jnp.where(same_place(shape), 1.0, 0.0)


def energy_here():
    index = lax.axis_index("energy")
    return LOWEST + SPREAD * (index.astype(F32) + 0.5) / lax.axis_size("energy")


def upright(x):
    size = x.shape[1]
    wide = jnp.broadcast_to(x, (size, size))
    return jnp.sum(jnp.where(same_place(wide.shape), wide, jnp.zeros_like(wide)), axis=1, keepdims=True)


def bound_kernel(*refs):
    sources, (first_out, second_out, start_out, term) = refs[:5], refs[5:9]
    onsite, coupling, bound, hopping, sigma = places = refs[9:14]
    arrived = refs[14]
    size, few = hopping.shape[0], coupling.shape[1]
    copies = [
        pltpu.make_async_copy(source, target, arrived.at[at])
        for at, (source, target) in enumerate(zip(sources[:3], places[:3]))
    ]
    chunks = []
    for row in range(0, size, TILE):
        at = len(copies) + 2 * len(chunks)
        part = pl.ds(row, TILE)
        chunks.append(
            [
                pltpu.make_async_copy(sources[3].at[part], hopping.at[part], arrived.at[at]),
                pltpu.make_async_copy(sources[4].at[:, part], sigma.at[:, part], arrived.at[at + 1]),
            ]
        )
    for copy in [*copies, *sum(chunks, [])]:
        copy.start()
    for copy in copies:
        copy.wait()
    level = energy_here() - onsite[...]
    pieces, start = [], []
    for at, chunk in enumerate(chunks):
        for copy in chunk:
            copy.wait()
        row = at * TILE
        rows = lax.broadcasted_iota(jnp.int32, (TILE, size), 0) + row
        diagonal = rows == lax.broadcasted_iota(jnp.int32, (TILE, size), 1)
        real = jnp.where(diagonal, level, 0.0) - hopping[row : row + TILE] - sigma[0, row : row + TILE]
        imag = jnp.where(diagonal, BROADENING, 0.0) - sigma[1, row : row + TILE]
        down, across = start_of(real, imag, row)
        start.append(across)
        piece = remainder(real, imag, down, row)
        first_out[row : row + TILE] = piece
        high, low = split(piece)
        pieces.append((high, low))
    start = [jnp.concatenate(part, axis=1) for part in zip(*start)]
    start_out[0:1] = start[0]
    start_out[1:2] = start[1]
    high, low = [jnp.concatenate(part, axis=0) for part in zip(*pieces)]
    second = dot(
        jnp.concatenate([high, high, low], axis=1),
        jnp.concatenate([high, turned(high), low, turned(low), high, turned(high)], axis=0),
    )
    second_out[...] = second
    here = bound[...]
    chosen = lax.broadcasted_iota(jnp.int32, (size, few), 0) == here
    narrow = [
        jnp.sum(jnp.where(chosen, jnp.broadcast_to(upright(x), chosen.shape), 0.0), axis=0, keepdims=True)
        for x in start
    ]
    some = columns_of(high, low, here)
    some = some + jnp.concatenate([jnp.where(chosen, 1.0, 0.0), jnp.zeros_like(some[:, few:])], axis=1)
    some = column_scaled(some, narrow)
    left = left_of(second)
    some = some + dot(left, right_of(some))
    some = some + dot(left, right_of(dot(left, right_of(some))))
    strength = coupling[...]
    term[...] = rows_of(*split(some), here) * upright(strength) * twice(strength)


def slab_kernel(first, second, start, top, bottom, fourth):
    size, half = first.shape[0], top.shape[0]
    one, two = first[...], second[...]
    both = dot(jnp.concatenate([left_of(one), left_of(two)], axis=0), right_of(two))
    total = unit(one.shape) + one + two + both[:size]
    fourth[...] = both[size:]
    bottom[...] = total[half:]
    scale = (start[0:1], start[1:2])
    top[...] = column_scaled(total[:half] + product(total[:half], both[size:]), scale)


def edge_kernel(top, partial, fourth, start, coupling, bound, bottom, columns, rows):
    total = partial[...]
    lower = column_scaled(total + product(total, fourth[...]), (start[0:1], start[1:2]))
    bottom[...] = lower
    high, low = split(jnp.concatenate([top[...], lower], axis=0))
    here, strength = bound[...], coupling[...]
    columns[...] = columns_of(high, low, here) * twice(strength)
    rows[...] = rows_of(high, low, here) * upright(strength)


def green_kernel(hamiltonian, top, bottom, columns, rows, near, far, *greens):
    few = hamiltonian.shape[0]
    schur = near[...] + far[...]
    diagonal = same_place(hamiltonian.shape)
    real = jnp.where(diagonal, energy_here(), 0.0) - hamiltonian[...] - schur[:, :few]
    imag = jnp.where(diagonal, BROADENING, 0.0) - schur[:, few:]
    down, across = start_of(real, imag, 0)
    first = remainder(real, imag, down, 0)
    second = product(first, first)
    both = dot(jnp.concatenate([left_of(first), left_of(second)], axis=0), right_of(second))
    total = unit(first.shape) + first + second + both[:few]
    separator = column_scaled(total + product(total, both[few:]), across)
    middle = product(columns[...], separator)
    change = product(middle, rows[...])
    half, size = greens[0].shape
    for at in (0, 1):
        for side, inverse in enumerate((top, bottom)):
            part = (slice(None), slice(at * size, (at + 1) * size))
            greens[2 * at + side][...] = inverse[part] + change[side * half : (side + 1) * half][part]


def strengths(steps, weights):
    absorb, emit = [], []
    for distance in (1, 2):
        for row, out in ((0, absorb), (1, emit)):
            total = jnp.float32(0.0)
            for mode in range(steps.shape[0]):
                total = total + jnp.where(steps[mode] == distance, weights[row, mode], 0.0)
            out.append(total)
    return absorb, emit


def place():
    energy, count = lax.axis_index("energy"), lax.axis_size("energy")
    odd = lax.rem(energy, 2) == 1
    odd_pair = lax.rem(lax.div(energy, 2), 2) == 1
    lower, higher = energy >= 2, energy + 2 < count
    one = jnp.where(odd_pair, lower.astype(jnp.int32), higher.astype(jnp.int32)) == 1
    two = jnp.where(odd_pair, higher.astype(jnp.int32), lower.astype(jnp.int32)) == 1
    return odd, odd_pair, one, two


def kept(there, x):
    return jnp.where(there, x, jnp.zeros_like(x))


def combine_kernel(steps, weights, green_a, green_b, one_a, two_a, pair_b, across_a, one_b, two_b):
    absorb, emit = strengths(steps, weights)
    odd, odd_pair, one, two = place()
    zero = jnp.float32(0.0)
    from_one = jnp.where(odd, jnp.where(odd_pair, absorb[0], zero), jnp.where(odd_pair, zero, emit[0]))
    from_two = jnp.where(odd, jnp.where(odd_pair, zero, absorb[0]), jnp.where(odd_pair, emit[0], zero))
    across_a[...] = (
        jnp.where(odd, emit[0], absorb[0]) * green_a[...]
        + from_one * kept(one, one_a[...])
        + from_two * kept(two, two_a[...])
    )
    up = (absorb[1], jnp.where(odd, zero, absorb[0]))
    down = (emit[1], jnp.where(odd, emit[0], zero))
    for out, first, second in ((one_b, up, down), (two_b, down, up)):
        own, other = [jnp.where(odd_pair, b, a) for a, b in zip(first, second)]
        out[...] = own * green_b[...] + other * pair_b[...]


def dress_kernel(steps, weights, vertex_left, vertex_right, one_a, two_a, across_a, one_b, two_b, pair_b, *rest):
    out = rest[-1]
    absorb, emit = strengths(steps, weights)
    odd, odd_pair, one, two = place()
    from_one = jnp.where(odd_pair, absorb[1], emit[1])
    from_two = jnp.where(odd_pair, emit[1], absorb[1])
    mixed_a = from_one * kept(one, one_a[...]) + from_two * kept(two, two_a[...]) + across_a[...]
    mixed_b = (
        kept(one, one_b[...]) + kept(two, two_b[...]) + jnp.where(odd, absorb[0], emit[0]) * pair_b[...]
    )
    mixed = jnp.concatenate([mixed_a, mixed_b], axis=0)
    high, low = split(mixed)
    inner = dot(vertex_left[...], jnp.concatenate([high, low, high], axis=0))
    high, low = split(inner)
    out[0] = dot(jnp.concatenate([high, high, low], axis=1), vertex_right[...])


def vertex_kernel(vertex, left, right):
    size = vertex.shape[0]
    high, low = split(vertex[...])
    for at, part in enumerate((high, high, low)):
        left[:, at * size : (at + 1) * size] = part
    high, low = split(vertex[...].T)
    for at, part in enumerate((high, low, high)):
        right[at * size : (at + 1) * size, :] = part


def call(kernel, outs, args, scalars=0, flops=0, **kept):
    vmem = pl.BlockSpec(memory_space=pltpu.VMEM)
    smem = pl.BlockSpec(memory_space=pltpu.SMEM)
    touched = sum(4 * a.size for a in [*args, *jax.tree.leaves(outs)])
    settings = dict(
        in_specs=[smem] * scalars + [vmem] * (len(args) - scalars),
        out_specs=jax.tree.map(lambda _: vmem, outs),
    )
    settings.update(kept)
    return pl.pallas_call(
        kernel,
        out_shape=outs,
        compiler_params=pltpu.CompilerParams(vmem_limit_bytes=VMEM_BYTES),
        cost_estimate=pl.CostEstimate(flops=flops, bytes_accessed=touched, transcendentals=0),
        **settings,
    )(*args)


def held(*shape):
    return jax.ShapeDtypeStruct(shape, F32)


def exchange(x, partner):
    slabs, energies = lax.axis_size("slab"), lax.axis_size("energy")
    pairs = []
    for slab in range(slabs):
        for energy in range(energies):
            other = partner(energy)
            if 0 <= other < energies:
                target = slab * energies + other
            else:
                target = (slab ^ 1) % slabs * energies + energy
            pairs.append((slab * energies + energy, target))
    return lax.ppermute(x, ("slab", "energy"), pairs)


def in_pair(energy):
    return energy ^ 1


def in_one(energy):
    return energy ^ 2


def in_two(energy):
    return energy + 2 if energy // 2 % 2 == 1 else energy - 2


def per_device(
    onsite,
    hopping,
    separator_hamiltonian,
    coupling,
    bound_rows,
    old_sigma,
    phonon_vertex,
    mode_steps,
    mode_weights,
):
    size, few = hopping.shape[-1], coupling.shape[-1]
    energies, slabs = lax.axis_size("energy"), lax.axis_size("slab")
    assert energies % 2 == 0 and slabs & (slabs - 1) == 0
    half = size // 2
    cube = 3 * 8 * size**3
    full = held(size, 2 * size)
    sigma = old_sigma.reshape(2, size, size)
    given = [
        pltpu.with_memory_space_constraint(x, pltpu.HBM)
        for x in (onsite, coupling, bound_rows, hopping[0], sigma)
    ]
    first, second, start, term = call(
        bound_kernel,
        [full, full, held(2, size), held(few, 2 * few)],
        given,
        flops=2 * cube,
        in_specs=[pl.BlockSpec(memory_space=pltpu.HBM)] * len(given),
        scratch_shapes=[pltpu.VMEM(x.shape, x.dtype) for x in given]
        + [pltpu.SemaphoreType.DMA((3 + 2 * (size // TILE),))],
    )
    part = held(half, 2 * size)
    top, bottom, fourth = call(slab_kernel, [part, part, full], [first, second, start], flops=5 * cube // 2)
    near, far, reach = term, None, slabs // 2
    while reach:
        if far is not None:
            far, top = lax.optimization_barrier((far, top))
            near = near + far
        far = lax.ppermute(near, "slab", [(i, i ^ reach) for i in range(slabs)])
        reach //= 2
    bottom, columns, rows = call(
        edge_kernel,
        [part, held(size, 2 * few), held(few, 2 * size)],
        [top, bottom, fourth, start, coupling, bound_rows],
        flops=cube // 2,
    )
    greens = call(
        green_kernel,
        [held(half, size)] * 4,
        [separator_hamiltonian, top, bottom, columns, rows, near, far],
        flops=cube,
    )
    parts = []
    for green_a, green_b in (greens[:2], greens[2:]):
        two_a = exchange(green_a, in_two)
        one_a = exchange(green_a, in_one)
        pair_b = exchange(green_b, in_pair)
        parts.append((green_a, green_b, one_a, two_a, pair_b))
    combined = []
    for part in parts:
        across_a, one_b, two_b = call(
            combine_kernel,
            [held(half, size)] * 3,
            [mode_steps, mode_weights, *part],
            scalars=2,
        )
        two_b = exchange(two_b, in_two)
        one_b = exchange(one_b, in_one)
        across_a = exchange(across_a, in_pair)
        combined.append((across_a, one_b, two_b))
    vertex = call(
        vertex_kernel,
        [jax.ShapeDtypeStruct((size, 3 * size), BF16), jax.ShapeDtypeStruct((3 * size, size), BF16)],
        [phonon_vertex[0]],
    )
    out = None
    for at, (part, more) in enumerate(zip(parts, combined)):
        args = [mode_steps, mode_weights, *vertex, part[2], part[3], *more, part[4]]
        vmem = pl.BlockSpec(memory_space=pltpu.VMEM)
        specs = [pl.BlockSpec(memory_space=pltpu.SMEM)] * 2 + [vmem] * (len(args) - 2)
        aliases = {}
        if out is not None:
            aliases = {len(args): 0}
            args, specs = [*args, out], [*specs, pl.BlockSpec(memory_space=pl.ANY)]
        out = call(
            dress_kernel,
            held(2, size, size),
            args,
            flops=cube // 4,
            in_specs=specs,
            grid=(1,),
            out_specs=pl.BlockSpec((1, size, size), functools.partial(lambda at, i: (at, 0, 0), at)),
            input_output_aliases=aliases,
        )
    return out.reshape(old_sigma.shape)


def solution(mesh):
    placed = (
        P("slab", None),
        P("slab", None, None),
        P(),
        P("slab", None),
        P("slab", None),
        P(None, "energy", "slab", None, None),
        P("slab", None, None),
        P(),
        P(),
    )
    return jax.shard_map(
        per_device,
        mesh=mesh,
        in_specs=placed,
        out_specs=P(None, "energy", "slab", None, None),
        check_vma=False,
    )
```

```python
import functools

import jax
import jax.numpy as jnp
from jax import lax
from jax.experimental import pallas as pl
from jax.experimental.pallas import tpu as pltpu
from jax.sharding import PartitionSpec as P

BROADENING = 1.0
LOWEST = -2.0
SPREAD = 4.0

F32 = jnp.float32
BF16 = jnp.bfloat16
VMEM_BYTES = 24 << 20


def split(x):
    high = x.astype(BF16)
    return high, (x - high.astype(F32)).astype(BF16)


def turned(x):
    half = x.shape[1] // 2
    return jnp.concatenate([-x[:, half:], x[:, :half]], axis=1)


def left_of(x):
    high, low = split(x)
    return jnp.concatenate([high, high, low], axis=1)


def right_of(x):
    high, low = split(x)
    high = jnp.concatenate([high, turned(high)], axis=0)
    low = jnp.concatenate([low, turned(low)], axis=0)
    return jnp.concatenate([high, low, high], axis=0)


def dot(a, b):
    return jnp.dot(a, b, preferred_element_type=F32)


def product(a, b):
    return dot(left_of(a), right_of(b))


def column_scaled(x, factor):
    half = x.shape[1] // 2
    real, imag = x[:, :half], x[:, half:]
    return jnp.concatenate(
        [real * factor[0] - imag * factor[1], imag * factor[0] + real * factor[1]], axis=1
    )


def stacked(x):
    half = x.shape[1] // 2
    return jnp.concatenate([x[:, :half], x[:, half:]], axis=0)


def beside(x):
    half = x.shape[0] // 2
    return jnp.concatenate([x[:half], x[half:]], axis=1)


def columns_of(high, low, places):
    rows = lax.broadcasted_iota(jnp.int32, (high.shape[1] // 2, places.shape[1]), 0)
    pick = (rows == places).astype(F32).astype(BF16)
    return beside(dot(stacked(high), pick) + dot(stacked(low), pick))


def rows_of(high, low, places):
    shape = (places.shape[1], high.shape[0])
    pick = lax.broadcasted_iota(jnp.int32, shape, 1) == upright(places.astype(F32)).astype(jnp.int32)
    pick = pick.astype(F32).astype(BF16)
    return dot(pick, high) + dot(pick, low)


def twice(row):
    return jnp.concatenate([row, row], axis=1)


def same_place(shape):
    rows = lax.broadcasted_iota(jnp.int32, shape, 0)
    cols = lax.broadcasted_iota(jnp.int32, shape, 1)
    return rows == cols


def reciprocal(real, imag):
    magnitude = real * real + imag * imag
    return real / magnitude, -imag / magnitude


TILE = 128


def start_of(real, imag, row):
    count = real.shape[0]
    blocks = [x[:, row : row + count] for x in (real, imag)]
    diagonal = same_place(blocks[0].shape)
    blocks = [jnp.where(diagonal, x, jnp.zeros_like(x)) for x in blocks]
    return [
        reciprocal(*[jnp.sum(x, axis=axis, keepdims=True) for x in blocks]) for axis in (1, 0)
    ]


def remainder(real, imag, down, row):
    rows = lax.broadcasted_iota(jnp.int32, real.shape, 0) + row
    off = rows != lax.broadcasted_iota(jnp.int32, real.shape, 1)
    zero = jnp.zeros_like(real)
    return jnp.concatenate(
        [
            jnp.where(off, down[1] * imag - down[0] * real, zero),
            jnp.where(off, -(down[1] * real) - down[0] * imag, zero),
        ],
        axis=1,
    )


def unit(shape):
    return jnp.where(same_place(shape), 1.0, 0.0)


def energy_here():
    index = lax.axis_index("energy")
    return LOWEST + SPREAD * (index.astype(F32) + 0.5) / lax.axis_size("energy")


def upright(x):
    size = x.shape[1]
    wide = jnp.broadcast_to(x, (size, size))
    return jnp.sum(jnp.where(same_place(wide.shape), wide, jnp.zeros_like(wide)), axis=1, keepdims=True)


def bound_kernel(*refs):
    sources, (first_out, second_out, start_out, term) = refs[:5], refs[5:9]
    onsite, coupling, bound, hopping, sigma = places = refs[9:14]
    arrived = refs[14]
    size, few = hopping.shape[0], coupling.shape[1]
    copies = [
        pltpu.make_async_copy(source, target, arrived.at[at])
        for at, (source, target) in enumerate(zip(sources[:3], places[:3]))
    ]
    chunks = []
    for row in range(0, size, TILE):
        at = len(copies) + 2 * len(chunks)
        part = pl.ds(row, TILE)
        chunks.append(
            [
                pltpu.make_async_copy(sources[3].at[part], hopping.at[part], arrived.at[at]),
                pltpu.make_async_copy(sources[4].at[:, part], sigma.at[:, part], arrived.at[at + 1]),
            ]
        )
    for copy in [*copies, *sum(chunks, [])]:
        copy.start()
    for copy in copies:
        copy.wait()
    level = energy_here() - onsite[...]
    pieces, start = [], []
    for at, chunk in enumerate(chunks):
        for copy in chunk:
            copy.wait()
        row = at * TILE
        rows = lax.broadcasted_iota(jnp.int32, (TILE, size), 0) + row
        diagonal = rows == lax.broadcasted_iota(jnp.int32, (TILE, size), 1)
        real = jnp.where(diagonal, level, 0.0) - hopping[row : row + TILE] - sigma[0, row : row + TILE]
        imag = jnp.where(diagonal, BROADENING, 0.0) - sigma[1, row : row + TILE]
        down, across = start_of(real, imag, row)
        start.append(across)
        piece = remainder(real, imag, down, row)
        first_out[row : row + TILE] = piece
        high, low = split(piece)
        pieces.append((high, low))
    start = [jnp.concatenate(part, axis=1) for part in zip(*start)]
    start_out[0:1] = start[0]
    start_out[1:2] = start[1]
    high, low = [jnp.concatenate(part, axis=0) for part in zip(*pieces)]
    second = dot(
        jnp.concatenate([high, high, low], axis=1),
        jnp.concatenate([high, turned(high), low, turned(low), high, turned(high)], axis=0),
    )
    second_out[...] = second
    here = bound[...]
    chosen = lax.broadcasted_iota(jnp.int32, (size, few), 0) == here
    narrow = [
        jnp.sum(jnp.where(chosen, jnp.broadcast_to(upright(x), chosen.shape), 0.0), axis=0, keepdims=True)
        for x in start
    ]
    some = rows_of(*split(unit(second.shape) + first_out[...]), here)
    right = right_of(second)
    more = dot(left_of(some), right)
    most = more + dot(left_of(more), right)
    some = columns_of(*split(some + more), here) + product(most, columns_of(*split(second), here))
    some = column_scaled(some, narrow)
    strength = coupling[...]
    term[...] = some * upright(strength) * twice(strength)


def power_kernel(first, second, partial, fourth):
    size = first.shape[0]
    one, two = first[...], second[...]
    both = dot(jnp.concatenate([left_of(one), left_of(two)], axis=0), right_of(two))
    partial[...] = unit(one.shape) + one + two + both[:size]
    fourth[...] = both[size:]


def slab_kernel(partial, fourth, start, coupling, bound, inverse, columns, rows):
    total = partial[...]
    total = column_scaled(total + product(total, fourth[...]), (start[0:1], start[1:2]))
    inverse[...] = total
    high, low = split(total)
    here, strength = bound[...], coupling[...]
    columns[...] = columns_of(high, low, here) * twice(strength)
    rows[...] = rows_of(high, low, here) * upright(strength)


def green_kernel(hamiltonian, inverse, columns, rows, near, far, *greens):
    few = hamiltonian.shape[0]
    schur = near[...] + far[...]
    diagonal = same_place(hamiltonian.shape)
    real = jnp.where(diagonal, energy_here(), 0.0) - hamiltonian[...] - schur[:, :few]
    imag = jnp.where(diagonal, BROADENING, 0.0) - schur[:, few:]
    down, across = start_of(real, imag, 0)
    first = remainder(real, imag, down, 0)
    second = product(first, first)
    both = dot(jnp.concatenate([left_of(first), left_of(second)], axis=0), right_of(second))
    total = unit(first.shape) + first + second + both[:few]
    separator = column_scaled(total + product(total, both[few:]), across)
    middle = product(columns[...], separator)
    green = inverse[...] + product(middle, rows[...])
    half, size = greens[0].shape
    for at, part in enumerate((green[:, :size], green[:, size:])):
        greens[2 * at][...] = part[:half]
        greens[2 * at + 1][...] = part[half:]


def strengths(steps, weights):
    absorb, emit = [], []
    for distance in (1, 2):
        for row, out in ((0, absorb), (1, emit)):
            total = jnp.float32(0.0)
            for mode in range(steps.shape[0]):
                total = total + jnp.where(steps[mode] == distance, weights[row, mode], 0.0)
            out.append(total)
    return absorb, emit


def place():
    energy, count = lax.axis_index("energy"), lax.axis_size("energy")
    odd = lax.rem(energy, 2) == 1
    odd_pair = lax.rem(lax.div(energy, 2), 2) == 1
    lower, higher = energy >= 2, energy + 2 < count
    one = jnp.where(odd_pair, lower.astype(jnp.int32), higher.astype(jnp.int32)) == 1
    two = jnp.where(odd_pair, higher.astype(jnp.int32), lower.astype(jnp.int32)) == 1
    return odd, odd_pair, one, two


def kept(there, x):
    return jnp.where(there, x, jnp.zeros_like(x))


def combine_kernel(steps, weights, green_a, green_b, one_a, two_a, pair_b, across_a, one_b, two_b):
    absorb, emit = strengths(steps, weights)
    odd, odd_pair, one, two = place()
    zero = jnp.float32(0.0)
    from_one = jnp.where(odd, jnp.where(odd_pair, absorb[0], zero), jnp.where(odd_pair, zero, emit[0]))
    from_two = jnp.where(odd, jnp.where(odd_pair, zero, absorb[0]), jnp.where(odd_pair, emit[0], zero))
    across_a[...] = (
        jnp.where(odd, emit[0], absorb[0]) * green_a[...]
        + from_one * kept(one, one_a[...])
        + from_two * kept(two, two_a[...])
    )
    up = (absorb[1], jnp.where(odd, zero, absorb[0]))
    down = (emit[1], jnp.where(odd, emit[0], zero))
    for out, first, second in ((one_b, up, down), (two_b, down, up)):
        own, other = [jnp.where(odd_pair, b, a) for a, b in zip(first, second)]
        out[...] = own * green_b[...] + other * pair_b[...]


def dress_kernel(steps, weights, vertex_left, vertex_right, one_a, two_a, across_a, one_b, two_b, pair_b, *rest):
    out = rest[-1]
    absorb, emit = strengths(steps, weights)
    odd, odd_pair, one, two = place()
    from_one = jnp.where(odd_pair, absorb[1], emit[1])
    from_two = jnp.where(odd_pair, emit[1], absorb[1])
    mixed_a = from_one * kept(one, one_a[...]) + from_two * kept(two, two_a[...]) + across_a[...]
    mixed_b = (
        kept(one, one_b[...]) + kept(two, two_b[...]) + jnp.where(odd, absorb[0], emit[0]) * pair_b[...]
    )
    mixed = jnp.concatenate([mixed_a, mixed_b], axis=0)
    high, low = split(mixed)
    inner = dot(vertex_left[...], jnp.concatenate([high, low, high], axis=0))
    high, low = split(inner)
    out[0] = dot(jnp.concatenate([high, high, low], axis=1), vertex_right[...])


def vertex_kernel(vertex, left, right):
    size = vertex.shape[0]
    high, low = split(vertex[...])
    for at, part in enumerate((high, high, low)):
        left[:, at * size : (at + 1) * size] = part
    high, low = split(vertex[...].T)
    for at, part in enumerate((high, low, high)):
        right[at * size : (at + 1) * size, :] = part


def call(kernel, outs, args, scalars=0, flops=0, **kept):
    vmem = pl.BlockSpec(memory_space=pltpu.VMEM)
    smem = pl.BlockSpec(memory_space=pltpu.SMEM)
    touched = sum(4 * a.size for a in [*args, *jax.tree.leaves(outs)])
    settings = dict(
        in_specs=[smem] * scalars + [vmem] * (len(args) - scalars),
        out_specs=jax.tree.map(lambda _: vmem, outs),
    )
    settings.update(kept)
    return pl.pallas_call(
        kernel,
        out_shape=outs,
        compiler_params=pltpu.CompilerParams(vmem_limit_bytes=VMEM_BYTES),
        cost_estimate=pl.CostEstimate(flops=flops, bytes_accessed=touched, transcendentals=0),
        **settings,
    )(*args)


def held(*shape):
    return jax.ShapeDtypeStruct(shape, F32)


def exchange(x, partner):
    slabs, energies = lax.axis_size("slab"), lax.axis_size("energy")
    pairs = []
    for slab in range(slabs):
        for energy in range(energies):
            other = partner(energy)
            if 0 <= other < energies:
                target = slab * energies + other
            else:
                target = (slab ^ 1) % slabs * energies + energy
            pairs.append((slab * energies + energy, target))
    return lax.ppermute(x, ("slab", "energy"), pairs)


def in_pair(energy):
    return energy ^ 1


def in_one(energy):
    return energy ^ 2


def in_two(energy):
    return energy + 2 if energy // 2 % 2 == 1 else energy - 2


def per_device(
    onsite,
    hopping,
    separator_hamiltonian,
    coupling,
    bound_rows,
    old_sigma,
    phonon_vertex,
    mode_steps,
    mode_weights,
):
    size, few = hopping.shape[-1], coupling.shape[-1]
    energies, slabs = lax.axis_size("energy"), lax.axis_size("slab")
    assert energies % 2 == 0 and slabs & (slabs - 1) == 0
    half = size // 2
    cube = 3 * 8 * size**3
    full = held(size, 2 * size)
    sigma = old_sigma.reshape(2, size, size)
    given = [
        pltpu.with_memory_space_constraint(x, pltpu.HBM)
        for x in (onsite, coupling, bound_rows, hopping[0], sigma)
    ]
    first, second, start, term = call(
        bound_kernel,
        [full, full, held(2, size), held(few, 2 * few)],
        given,
        flops=2 * cube,
        in_specs=[pl.BlockSpec(memory_space=pltpu.HBM)] * len(given),
        scratch_shapes=[pltpu.VMEM(x.shape, x.dtype) for x in given]
        + [pltpu.SemaphoreType.DMA((3 + 2 * (size // TILE),))],
    )
    partial, fourth = call(power_kernel, [full, full], [first, second], flops=2 * cube)
    near, far, reach = term, None, slabs // 2
    while reach:
        if far is not None:
            far, fourth = lax.optimization_barrier((far, fourth))
            near = near + far
        far = lax.ppermute(near, "slab", [(i, i ^ reach) for i in range(slabs)])
        reach //= 2
    inverse, columns, rows = call(
        slab_kernel,
        [full, held(size, 2 * few), held(few, 2 * size)],
        [partial, fourth, start, coupling, bound_rows],
        flops=cube,
    )
    greens = call(
        green_kernel,
        [held(half, size)] * 4,
        [separator_hamiltonian, inverse, columns, rows, near, far],
        flops=cube,
    )
    parts = []
    for green_a, green_b in (greens[:2], greens[2:]):
        two_a = exchange(green_a, in_two)
        one_a = exchange(green_a, in_one)
        pair_b = exchange(green_b, in_pair)
        parts.append((green_a, green_b, one_a, two_a, pair_b))
    combined = []
    for part in parts:
        across_a, one_b, two_b = call(
            combine_kernel,
            [held(half, size)] * 3,
            [mode_steps, mode_weights, *part],
            scalars=2,
        )
        two_b = exchange(two_b, in_two)
        one_b = exchange(one_b, in_one)
        across_a = exchange(across_a, in_pair)
        combined.append((across_a, one_b, two_b))
    vertex = call(
        vertex_kernel,
        [jax.ShapeDtypeStruct((size, 3 * size), BF16), jax.ShapeDtypeStruct((3 * size, size), BF16)],
        [phonon_vertex[0]],
    )
    out = None
    for at, (part, more) in enumerate(zip(parts, combined)):
        args = [mode_steps, mode_weights, *vertex, part[2], part[3], *more, part[4]]
        vmem = pl.BlockSpec(memory_space=pltpu.VMEM)
        specs = [pl.BlockSpec(memory_space=pltpu.SMEM)] * 2 + [vmem] * (len(args) - 2)
        aliases = {}
        if out is not None:
            aliases = {len(args): 0}
            args, specs = [*args, out], [*specs, pl.BlockSpec(memory_space=pl.ANY)]
        out = call(
            dress_kernel,
            held(2, size, size),
            args,
            flops=cube // 4,
            in_specs=specs,
            grid=(1,),
            out_specs=pl.BlockSpec((1, size, size), functools.partial(lambda at, i: (at, 0, 0), at)),
            input_output_aliases=aliases,
        )
    return out.reshape(old_sigma.shape)


def solution(mesh):
    placed = (
        P("slab", None),
        P("slab", None, None),
        P(),
        P("slab", None),
        P("slab", None),
        P(None, "energy", "slab", None, None),
        P("slab", None, None),
        P(),
        P(),
    )
    return jax.shard_map(
        per_device,
        mesh=mesh,
        in_specs=placed,
        out_specs=P(None, "energy", "slab", None, None),
        check_vma=False,
    )
```

```python
import functools

import jax
import jax.numpy as jnp
from jax import lax
from jax.experimental import pallas as pl
from jax.experimental.pallas import tpu as pltpu
from jax.sharding import PartitionSpec as P


BROADENING = 1.0
LOWEST = -2.0
SPREAD = 4.0

F32 = jnp.float32
BF16 = jnp.bfloat16
VMEM_BYTES = 24 << 20


def split(x):
    high = x.astype(BF16)
    return high, (x - high.astype(F32)).astype(BF16)


def turned(x):
    half = x.shape[1] // 2
    return jnp.concatenate([-x[:, half:], x[:, :half]], axis=1)


def left_of(x):
    high, low = split(x)
    return jnp.concatenate([high, high, low], axis=1)


def right_of(x):
    high, low = split(x)
    high = jnp.concatenate([high, turned(high)], axis=0)
    low = jnp.concatenate([low, turned(low)], axis=0)
    return jnp.concatenate([high, low, high], axis=0)


def dot(a, b):
    return jnp.dot(a, b, preferred_element_type=F32)


def product(a, b):
    return dot(left_of(a), right_of(b))


def row_scaled(factor, x):
    half = x.shape[1] // 2
    real, imag = x[:, :half], x[:, half:]
    return jnp.concatenate(
        [factor[0] * real - factor[1] * imag, factor[0] * imag + factor[1] * real], axis=1
    )


def same_place(shape):
    rows = lax.broadcasted_iota(jnp.int32, shape, 0)
    cols = lax.broadcasted_iota(jnp.int32, shape, 1)
    return rows == cols


def reciprocal(real, imag):
    magnitude = real * real + imag * imag
    return real / magnitude, -imag / magnitude


def reciprocal_diagonal(real, imag):
    tile = 128
    ways = ([], [])
    for at in range(0, real.shape[0], tile):
        blocks = [x[at : at + tile, at : at + tile] for x in (real, imag)]
        diagonal = same_place(blocks[0].shape)
        blocks = [jnp.where(diagonal, x, jnp.zeros_like(x)) for x in blocks]
        for axis in (0, 1):
            ways[axis].append([jnp.sum(x, axis=axis, keepdims=True) for x in blocks])
    across = [jnp.concatenate(part, axis=1) for part in zip(*ways[0])]
    down = [jnp.concatenate(part, axis=0) for part in zip(*ways[1])]
    return reciprocal(*across), reciprocal(*down)


def remainder(real, imag, across):
    diagonal = same_place(real.shape)
    zero = jnp.zeros_like(real)
    return jnp.concatenate(
        [
            jnp.where(diagonal, zero, imag * across[1] - real * across[0]),
            jnp.where(diagonal, zero, -(real * across[1]) - imag * across[0]),
        ],
        axis=1,
    )


def unit(shape):
    return jnp.where(same_place(shape), 1.0, 0.0)


def energy_here():
    index = lax.axis_index("energy")
    return LOWEST + SPREAD * (index.astype(F32) + 0.5) / lax.axis_size("energy")


def upright(x):
    size = x.shape[1]
    wide = jnp.broadcast_to(x, (size, size))
    return jnp.sum(jnp.where(same_place(wide.shape), wide, jnp.zeros_like(wide)), axis=1, keepdims=True)


def bound_kernel(*refs):
    sources, outs = refs[:5], refs[5:10]
    onsite, hopping, sigma, coupling, bound = places = refs[10:15]
    first_out, second_out, start_out, rows, term = outs
    arrived = refs[15]
    copies = [
        pltpu.make_async_copy(source, target, arrived.at[at])
        for at, (source, target) in enumerate(zip(sources, places))
    ]
    for copy in copies:
        copy.start()
    for copy in copies:
        copy.wait()
    size, few = hopping.shape[0], coupling.shape[1]
    diagonal = same_place(hopping.shape)
    level = energy_here() - onsite[...]
    real = jnp.where(diagonal, level, 0.0) - hopping[...] - sigma[0]
    imag = jnp.where(diagonal, BROADENING, 0.0) - sigma[1]
    across, down = reciprocal_diagonal(real, imag)
    first = remainder(real, imag, across)
    first_out[...] = first
    start_out[...] = jnp.concatenate(down, axis=1)
    second = product(first, first)
    second_out[...] = second
    places = bound[...]
    pick_rows = (
        lax.broadcasted_iota(jnp.int32, (few, size), 1) == upright(places.astype(F32)).astype(jnp.int32)
    ).astype(F32).astype(BF16)
    pick_cols = (lax.broadcasted_iota(jnp.int32, (size, few), 0) == places).astype(F32).astype(BF16)
    strength = coupling[...]
    high, low = split(row_scaled(down, unit(first.shape) + first))
    some = dot(pick_rows, high) + dot(pick_rows, low)
    right = right_of(second)
    some = some + dot(left_of(some), right)
    some = some + dot(left_of(dot(left_of(some), right)), right)
    some = some * upright(strength)
    rows[...] = some
    high, low = split(jnp.concatenate([some[:, :size], some[:, size:]], axis=0))
    corner = dot(high, pick_cols) + dot(low, pick_cols)
    corner = corner * strength
    term[...] = jnp.concatenate([corner[:few], corner[few:]], axis=1)


def power_kernel(first, second, start, partial, fourth):
    size = first.shape[0]
    one, two = first[...], second[...]
    both = dot(jnp.concatenate([left_of(one), left_of(two)], axis=0), right_of(two))
    total = unit(one.shape) + one + two + both[:size]
    partial[...] = row_scaled((start[:, 0:1], start[:, 1:2]), total)
    fourth[...] = both[size:]


def slab_kernel(partial, fourth, inverse):
    inverse[...] = partial[...] + product(partial[...], fourth[...])


def columns_of(x, places):
    size = x.shape[1] // 2
    pick = lax.broadcasted_iota(jnp.int32, (size, places.shape[1]), 0) == places
    pick = pick.astype(F32).astype(BF16)
    high, low = split(jnp.concatenate([x[:, :size], x[:, size:]], axis=0))
    chosen = dot(jnp.concatenate([high, low], axis=1), jnp.concatenate([pick, pick], axis=0))
    return jnp.concatenate([chosen[: x.shape[0]], chosen[x.shape[0] :]], axis=1)


def green_kernel(hamiltonian, coupling, bound, inverse, rows, near, far, middle, green_a, green_b):
    few = hamiltonian.shape[0]
    strength = coupling[...]
    columns = columns_of(inverse[...], bound[...]) * jnp.concatenate([strength, strength], axis=1)
    schur = near[...] + far[...]
    diagonal = same_place(hamiltonian.shape)
    real = jnp.where(diagonal, energy_here(), 0.0) - hamiltonian[...] - schur[:, :few]
    imag = jnp.where(diagonal, BROADENING, 0.0) - schur[:, few:]
    across, down = reciprocal_diagonal(real, imag)
    first = remainder(real, imag, across)
    second = product(first, first)
    both = dot(jnp.concatenate([left_of(first), left_of(second)], axis=0), right_of(second))
    total = row_scaled(down, unit(first.shape) + first + second + both[:few])
    separator = total + product(total, both[few:])
    inner = product(columns, separator)
    middle[...] = inner
    half, size = green_a.shape
    green = inverse[:, :size] + dot(left_of(inner), right_of(rows[...])[:, :size])
    green_a[...] = green[:half]
    green_b[...] = green[half:]


def imaginary_kernel(middle, rows, inverse, green_a, green_b):
    half, size = green_a.shape
    green = inverse[:, size:] + dot(left_of(middle[...]), right_of(rows[...])[:, size:])
    green_a[...] = green[:half]
    green_b[...] = green[half:]


def strengths(steps, weights):
    absorb, emit = [], []
    for distance in (1, 2):
        for row, out in ((0, absorb), (1, emit)):
            total = jnp.float32(0.0)
            for mode in range(steps.shape[0]):
                total = total + jnp.where(steps[mode] == distance, weights[row, mode], 0.0)
            out.append(total)
    return absorb, emit


def place():
    energy, count = lax.axis_index("energy"), lax.axis_size("energy")
    odd = lax.rem(energy, 2) == 1
    odd_pair = lax.rem(lax.div(energy, 2), 2) == 1
    lower, higher = energy >= 2, energy + 2 < count
    one = jnp.where(odd_pair, lower.astype(jnp.int32), higher.astype(jnp.int32)) == 1
    two = jnp.where(odd_pair, higher.astype(jnp.int32), lower.astype(jnp.int32)) == 1
    return odd, odd_pair, one, two


def kept(there, x):
    return jnp.where(there, x, jnp.zeros_like(x))


def combine_kernel(steps, weights, green_a, green_b, one_a, two_a, pair_b, across_a, one_b, two_b):
    absorb, emit = strengths(steps, weights)
    odd, odd_pair, one, two = place()
    zero = jnp.float32(0.0)
    from_one = jnp.where(odd, jnp.where(odd_pair, absorb[0], zero), jnp.where(odd_pair, zero, emit[0]))
    from_two = jnp.where(odd, jnp.where(odd_pair, zero, absorb[0]), jnp.where(odd_pair, emit[0], zero))
    across_a[...] = (
        jnp.where(odd, emit[0], absorb[0]) * green_a[...]
        + from_one * kept(one, one_a[...])
        + from_two * kept(two, two_a[...])
    )
    up = (absorb[1], jnp.where(odd, zero, absorb[0]))
    down = (emit[1], jnp.where(odd, emit[0], zero))
    for out, first, second in ((one_b, up, down), (two_b, down, up)):
        own, other = [jnp.where(odd_pair, b, a) for a, b in zip(first, second)]
        out[...] = own * green_b[...] + other * pair_b[...]


def dressed(left, right, mixed):
    high, low = split(mixed)
    outer = dot(jnp.concatenate([high, high, low], axis=1), right[...])
    high, low = split(outer)
    return dot(left[...], jnp.concatenate([high, low, high], axis=0))


def dress_a_kernel(steps, weights, left, right, one_a, two_a, across_a, out):
    absorb, emit = strengths(steps, weights)
    _, odd_pair, one, two = place()
    from_one = jnp.where(odd_pair, absorb[1], emit[1])
    from_two = jnp.where(odd_pair, emit[1], absorb[1])
    mixed = from_one * kept(one, one_a[...]) + from_two * kept(two, two_a[...]) + across_a[...]
    out[...] = dressed(left, right, mixed)


def dress_b_kernel(steps, weights, left, right, one_b, two_b, pair_b, other, *rest):
    absorb, emit = strengths(steps, weights)
    odd, _, one, two = place()
    mixed = kept(one, one_b[...]) + kept(two, two_b[...]) + jnp.where(odd, absorb[0], emit[0]) * pair_b[...]
    out = rest[-1]
    out[0] = other[...] + dressed(left, right, mixed)


def vertex_left_kernel(vertex, left_a, left_b):
    half = left_a.shape[1] // 3
    high, low = split(vertex[...])
    for side, left in enumerate((left_a, left_b)):
        part = (slice(None), slice(side * half, side * half + half))
        left[...] = jnp.concatenate([high[part], high[part], low[part]], axis=1)


def vertex_right_kernel(vertex, right):
    size = vertex.shape[0]
    high, low = split(vertex[...].T)
    for at, part in enumerate((high, low, high)):
        right[at * size : (at + 1) * size, :] = part


def call(kernel, outs, args, scalars=0, flops=0, **kept):
    vmem = pl.BlockSpec(memory_space=pltpu.VMEM)
    smem = pl.BlockSpec(memory_space=pltpu.SMEM)
    touched = sum(4 * a.size for a in [*args, *jax.tree.leaves(outs)])
    settings = dict(
        in_specs=[smem] * scalars + [vmem] * (len(args) - scalars),
        out_specs=jax.tree.map(lambda _: vmem, outs),
    )
    settings.update(kept)
    return pl.pallas_call(
        kernel,
        out_shape=outs,
        compiler_params=pltpu.CompilerParams(vmem_limit_bytes=VMEM_BYTES),
        cost_estimate=pl.CostEstimate(flops=flops, bytes_accessed=touched, transcendentals=0),
        **settings,
    )(*args)


def held(*shape):
    return jax.ShapeDtypeStruct(shape, F32)


def exchange(x, partner):
    slabs, energies = lax.axis_size("slab"), lax.axis_size("energy")
    pairs = []
    for slab in range(slabs):
        for energy in range(energies):
            other = partner(energy)
            if 0 <= other < energies:
                target = slab * energies + other
            else:
                target = (slab ^ 1) % slabs * energies + energy
            pairs.append((slab * energies + energy, target))
    return lax.ppermute(x, ("slab", "energy"), pairs)


def in_pair(energy):
    return energy ^ 1


def in_one(energy):
    return energy ^ 2


def in_two(energy):
    return energy + 2 if energy // 2 % 2 == 1 else energy - 2


def per_device(
    onsite,
    hopping,
    separator_hamiltonian,
    coupling,
    bound_rows,
    old_sigma,
    phonon_vertex,
    mode_steps,
    mode_weights,
):
    size, few = hopping.shape[-1], coupling.shape[-1]
    energies, slabs = lax.axis_size("energy"), lax.axis_size("slab")
    assert energies % 2 == 0 and slabs & (slabs - 1) == 0
    half = size // 2
    cube = 3 * 8 * size**3
    full = held(size, 2 * size)
    sigma = old_sigma.reshape(2, size, size)
    given = [
        pltpu.with_memory_space_constraint(x, pltpu.HBM)
        for x in (onsite, hopping[0], sigma, coupling, bound_rows)
    ]
    first, second, start, rows, term = call(
        bound_kernel,
        [full, full, held(size, 2), held(few, 2 * size), held(few, 2 * few)],
        given,
        flops=2 * cube,
        in_specs=[pl.BlockSpec(memory_space=pltpu.HBM)] * len(given),
        scratch_shapes=[pltpu.VMEM(x.shape, x.dtype) for x in given]
        + [pltpu.SemaphoreType.DMA((len(given),))],
    )
    partial, fourth = call(power_kernel, [full, full], [first, second, start], flops=2 * cube)
    near, far, reach = term, None, slabs // 2
    while reach:
        if far is not None:
            far, fourth = lax.optimization_barrier((far, fourth))
            near = near + far
        far = lax.ppermute(near, "slab", [(i, i ^ reach) for i in range(slabs)])
        reach //= 2
    inverse = call(slab_kernel, full, [partial, fourth], flops=cube)
    part = held(half, size)
    middle, *greens = call(
        green_kernel,
        [held(size, 2 * few), part, part],
        [separator_hamiltonian, coupling, bound_rows, inverse, rows, near, far],
        flops=cube,
    )
    parts = []
    for at in (0, 1):
        green_a, green_b = greens
        two_a = exchange(green_a, in_two)
        one_a = exchange(green_a, in_one)
        pair_b = exchange(green_b, in_pair)
        parts.append((green_a, green_b, one_a, two_a, pair_b))
        if at == 0:
            greens = call(imaginary_kernel, [part, part], [middle, rows, inverse], flops=cube // 4)
    combined = []
    for part in parts:
        across_a, one_b, two_b = call(
            combine_kernel, [held(half, size)] * 3, [mode_steps, mode_weights, *part], scalars=2
        )
        two_b = exchange(two_b, in_two)
        one_b = exchange(one_b, in_one)
        across_a = exchange(across_a, in_pair)
        combined.append((across_a, one_b, two_b))
    lefts = jax.ShapeDtypeStruct((size, 3 * half), BF16)
    left_a, left_b = call(vertex_left_kernel, [lefts, lefts], [phonon_vertex[0]])
    right = call(
        vertex_right_kernel, jax.ShapeDtypeStruct((3 * size, size), BF16), [phonon_vertex[0]]
    )
    out = None
    for at, (part, more) in enumerate(zip(parts, combined)):
        _, _, one_a, two_a, pair_b = part
        across_a, one_b, two_b = more
        other = call(
            dress_a_kernel,
            held(size, size),
            [mode_steps, mode_weights, left_a, right, one_a, two_a, across_a],
            scalars=2,
            flops=cube // 8,
        )
        args = [mode_steps, mode_weights, left_b, right, one_b, two_b, pair_b, other]
        vmem = pl.BlockSpec(memory_space=pltpu.VMEM)
        specs = [pl.BlockSpec(memory_space=pltpu.SMEM)] * 2 + [vmem] * (len(args) - 2)
        aliases = {}
        if out is not None:
            aliases = {len(args): 0}
            args, specs = [*args, out], [*specs, pl.BlockSpec(memory_space=pl.ANY)]
        out = call(
            dress_b_kernel,
            held(2, size, size),
            args,
            flops=cube // 8,
            in_specs=specs,
            grid=(1,),
            out_specs=pl.BlockSpec((1, size, size), functools.partial(lambda at, i: (at, 0, 0), at)),
            input_output_aliases=aliases,
        )
    return out.reshape(old_sigma.shape)


def solution(mesh):
    placed = (
        P("slab", None),
        P("slab", None, None),
        P(),
        P("slab", None),
        P("slab", None),
        P(None, "energy", "slab", None, None),
        P("slab", None, None),
        P(),
        P(),
    )

    return jax.shard_map(
        per_device,
        mesh=mesh,
        in_specs=placed,
        out_specs=P(None, "energy", "slab", None, None),
        check_vma=False,
    )
```

```python
import functools

import jax
import jax.numpy as jnp
from jax import lax
from jax.experimental import pallas as pl
from jax.experimental.pallas import tpu as pltpu
from jax.sharding import PartitionSpec as P


BROADENING = 1.0
LOWEST = -2.0
SPREAD = 4.0

F32 = jnp.float32
BF16 = jnp.bfloat16
VMEM_BYTES = 24 << 20


def split(x):
    high = x.astype(BF16)
    return high, (x - high.astype(F32)).astype(BF16)


def turned(x):
    half = x.shape[1] // 2
    return jnp.concatenate([-x[:, half:], x[:, :half]], axis=1)


def left_of(x):
    high, low = split(x)
    return jnp.concatenate([high, high, low], axis=1)


def right_of(x):
    high, low = split(x)
    high = jnp.concatenate([high, turned(high)], axis=0)
    low = jnp.concatenate([low, turned(low)], axis=0)
    return jnp.concatenate([high, low, high], axis=0)


def dot(a, b):
    return jnp.dot(a, b, preferred_element_type=F32)


def product(a, b):
    return dot(left_of(a), right_of(b))


def row_scaled(factor, x):
    half = x.shape[1] // 2
    real, imag = x[:, :half], x[:, half:]
    return jnp.concatenate(
        [factor[0] * real - factor[1] * imag, factor[0] * imag + factor[1] * real], axis=1
    )


def same_place(shape):
    rows = lax.broadcasted_iota(jnp.int32, shape, 0)
    cols = lax.broadcasted_iota(jnp.int32, shape, 1)
    return rows == cols


def reciprocal(real, imag):
    magnitude = real * real + imag * imag
    return real / magnitude, -imag / magnitude


def reciprocal_diagonal(real, imag):
    tile = 128
    ways = ([], [])
    for at in range(0, real.shape[0], tile):
        blocks = [x[at : at + tile, at : at + tile] for x in (real, imag)]
        diagonal = same_place(blocks[0].shape)
        blocks = [jnp.where(diagonal, x, jnp.zeros_like(x)) for x in blocks]
        for axis in (0, 1):
            ways[axis].append([jnp.sum(x, axis=axis, keepdims=True) for x in blocks])
    across = [jnp.concatenate(part, axis=1) for part in zip(*ways[0])]
    down = [jnp.concatenate(part, axis=0) for part in zip(*ways[1])]
    return reciprocal(*across), reciprocal(*down)


def remainder(real, imag, across):
    diagonal = same_place(real.shape)
    zero = jnp.zeros_like(real)
    return jnp.concatenate(
        [
            jnp.where(diagonal, zero, imag * across[1] - real * across[0]),
            jnp.where(diagonal, zero, -(real * across[1]) - imag * across[0]),
        ],
        axis=1,
    )


def unit(shape):
    return jnp.where(same_place(shape), 1.0, 0.0)


def energy_here():
    index = lax.axis_index("energy")
    return LOWEST + SPREAD * (index.astype(F32) + 0.5) / lax.axis_size("energy")


def upright(x):
    size = x.shape[1]
    wide = jnp.broadcast_to(x, (size, size))
    return jnp.sum(jnp.where(same_place(wide.shape), wide, jnp.zeros_like(wide)), axis=1, keepdims=True)


def bound_kernel(*refs):
    sources, outs = refs[:5], refs[5:10]
    onsite, hopping, sigma, coupling, bound = places = refs[10:15]
    first_out, second_out, start_out, rows, term = outs
    arrived = refs[15]
    copies = [
        pltpu.make_async_copy(source, target, arrived.at[at])
        for at, (source, target) in enumerate(zip(sources, places))
    ]
    for copy in copies:
        copy.start()
    for copy in copies:
        copy.wait()
    size, few = hopping.shape[0], coupling.shape[1]
    diagonal = same_place(hopping.shape)
    level = energy_here() - onsite[...]
    real = jnp.where(diagonal, level, 0.0) - hopping[...] - sigma[0]
    imag = jnp.where(diagonal, BROADENING, 0.0) - sigma[1]
    across, down = reciprocal_diagonal(real, imag)
    first = remainder(real, imag, across)
    first_out[...] = first
    start_out[...] = jnp.concatenate(down, axis=1)
    second = product(first, first)
    second_out[...] = second
    places = bound[...]
    pick_rows = (
        lax.broadcasted_iota(jnp.int32, (few, size), 1) == upright(places.astype(F32)).astype(jnp.int32)
    ).astype(F32).astype(BF16)
    pick_cols = (lax.broadcasted_iota(jnp.int32, (size, few), 0) == places).astype(F32).astype(BF16)
    strength = coupling[...]
    high, low = split(row_scaled(down, unit(first.shape) + first))
    some = dot(pick_rows, high) + dot(pick_rows, low)
    right = right_of(second)
    some = some + dot(left_of(some), right)
    some = some + dot(left_of(dot(left_of(some), right)), right)
    some = some * upright(strength)
    rows[...] = some
    high, low = split(jnp.concatenate([some[:, :size], some[:, size:]], axis=0))
    corner = dot(high, pick_cols) + dot(low, pick_cols)
    corner = corner * strength
    term[...] = jnp.concatenate([corner[:few], corner[few:]], axis=1)


def power_kernel(first, second, start, partial, fourth):
    size = first.shape[0]
    one, two = first[...], second[...]
    both = dot(jnp.concatenate([left_of(one), left_of(two)], axis=0), right_of(two))
    total = unit(one.shape) + one + two + both[:size]
    partial[...] = row_scaled((start[:, 0:1], start[:, 1:2]), total)
    fourth[...] = both[size:]


def slab_kernel(partial, fourth, inverse):
    inverse[...] = partial[...] + product(partial[...], fourth[...])


def columns_of(x, places):
    size = x.shape[1] // 2
    pick = lax.broadcasted_iota(jnp.int32, (size, places.shape[1]), 0) == places
    pick = pick.astype(F32).astype(BF16)
    high, low = split(jnp.concatenate([x[:, :size], x[:, size:]], axis=0))
    chosen = dot(jnp.concatenate([high, low], axis=1), jnp.concatenate([pick, pick], axis=0))
    return jnp.concatenate([chosen[: x.shape[0]], chosen[x.shape[0] :]], axis=1)


def green_kernel(hamiltonian, coupling, bound, inverse, rows, near, far, middle, green_a, green_b):
    few = hamiltonian.shape[0]
    strength = coupling[...]
    columns = columns_of(inverse[...], bound[...]) * jnp.concatenate([strength, strength], axis=1)
    schur = near[...] + far[...]
    diagonal = same_place(hamiltonian.shape)
    real = jnp.where(diagonal, energy_here(), 0.0) - hamiltonian[...] - schur[:, :few]
    imag = jnp.where(diagonal, BROADENING, 0.0) - schur[:, few:]
    across, down = reciprocal_diagonal(real, imag)
    first = remainder(real, imag, across)
    second = product(first, first)
    both = dot(jnp.concatenate([left_of(first), left_of(second)], axis=0), right_of(second))
    total = row_scaled(down, unit(first.shape) + first + second + both[:few])
    separator = total + product(total, both[few:])
    inner = product(columns, separator)
    middle[...] = inner
    half, size = green_a.shape
    green = inverse[:, :size] + dot(left_of(inner), right_of(rows[...])[:, :size])
    green_a[...] = green[:half]
    green_b[...] = green[half:]


def imaginary_kernel(middle, rows, inverse, green_a, green_b):
    half, size = green_a.shape
    green = inverse[:, size:] + dot(left_of(middle[...]), right_of(rows[...])[:, size:])
    green_a[...] = green[:half]
    green_b[...] = green[half:]


def strengths(steps, weights):
    absorb, emit = [], []
    for distance in (1, 2):
        for row, out in ((0, absorb), (1, emit)):
            total = jnp.float32(0.0)
            for mode in range(steps.shape[0]):
                total = total + jnp.where(steps[mode] == distance, weights[row, mode], 0.0)
            out.append(total)
    return absorb, emit


def place():
    energy, count = lax.axis_index("energy"), lax.axis_size("energy")
    odd = lax.rem(energy, 2) == 1
    odd_pair = lax.rem(lax.div(energy, 2), 2) == 1
    lower, higher = energy >= 2, energy + 2 < count
    one = jnp.where(odd_pair, lower.astype(jnp.int32), higher.astype(jnp.int32)) == 1
    two = jnp.where(odd_pair, higher.astype(jnp.int32), lower.astype(jnp.int32)) == 1
    return odd, odd_pair, one, two


def kept(there, x):
    return jnp.where(there, x, jnp.zeros_like(x))


def combine_kernel(steps, weights, green_a, green_b, one_a, two_a, pair_b, across_a, one_b, two_b):
    absorb, emit = strengths(steps, weights)
    odd, odd_pair, one, two = place()
    zero = jnp.float32(0.0)
    from_one = jnp.where(odd, jnp.where(odd_pair, absorb[0], zero), jnp.where(odd_pair, zero, emit[0]))
    from_two = jnp.where(odd, jnp.where(odd_pair, zero, absorb[0]), jnp.where(odd_pair, emit[0], zero))
    across_a[...] = (
        jnp.where(odd, emit[0], absorb[0]) * green_a[...]
        + from_one * kept(one, one_a[...])
        + from_two * kept(two, two_a[...])
    )
    up = (absorb[1], jnp.where(odd, zero, absorb[0]))
    down = (emit[1], jnp.where(odd, emit[0], zero))
    for out, first, second in ((one_b, up, down), (two_b, down, up)):
        own, other = [jnp.where(odd_pair, b, a) for a, b in zip(first, second)]
        out[...] = own * green_b[...] + other * pair_b[...]


def dress_kernel(at, steps, weights, left, right, one_a, two_a, across_a, one_b, two_b, pair_b, *rest):
    out, held_out, sent = rest[-3:]
    absorb, emit = strengths(steps, weights)
    odd, odd_pair, one, two = place()
    from_one = jnp.where(odd_pair, absorb[1], emit[1])
    from_two = jnp.where(odd_pair, emit[1], absorb[1])
    mixed_a = from_one * kept(one, one_a[...]) + from_two * kept(two, two_a[...]) + across_a[...]
    mixed_b = (
        kept(one, one_b[...]) + kept(two, two_b[...]) + jnp.where(odd, absorb[0], emit[0]) * pair_b[...]
    )
    high, low = split(jnp.concatenate([mixed_a, mixed_b], axis=0))
    high, low = split(dot(left[...], jnp.concatenate([high, low, high], axis=0)))
    outer = jnp.concatenate([high, high, low], axis=1)
    half = mixed_a.shape[0]
    copies = []
    for piece in (0, 1):
        rows = pl.ds(piece * half, half)
        held_out[rows] = dot(outer[piece * half : piece * half + half], right[...])
        copies.append(pltpu.make_async_copy(held_out.at[rows], out.at[at, rows], sent.at[piece]))
        copies[-1].start()
    for copy in copies:
        copy.wait()


def vertex_left_kernel(vertex, left):
    high, low = split(vertex[...])
    left[...] = jnp.concatenate([high, high, low], axis=1)


def vertex_right_kernel(vertex, right):
    size = vertex.shape[0]
    high, low = split(vertex[...].T)
    for at, part in enumerate((high, low, high)):
        right[at * size : (at + 1) * size, :] = part


def call(kernel, outs, args, scalars=0, flops=0, **kept):
    vmem = pl.BlockSpec(memory_space=pltpu.VMEM)
    smem = pl.BlockSpec(memory_space=pltpu.SMEM)
    touched = sum(4 * a.size for a in [*args, *jax.tree.leaves(outs)])
    settings = dict(
        in_specs=[smem] * scalars + [vmem] * (len(args) - scalars),
        out_specs=jax.tree.map(lambda _: vmem, outs),
    )
    settings.update(kept)
    return pl.pallas_call(
        kernel,
        out_shape=outs,
        compiler_params=pltpu.CompilerParams(vmem_limit_bytes=VMEM_BYTES),
        cost_estimate=pl.CostEstimate(flops=flops, bytes_accessed=touched, transcendentals=0),
        **settings,
    )(*args)


def held(*shape):
    return jax.ShapeDtypeStruct(shape, F32)


def exchange(x, partner):
    slabs, energies = lax.axis_size("slab"), lax.axis_size("energy")
    pairs = []
    for slab in range(slabs):
        for energy in range(energies):
            other = partner(energy)
            if 0 <= other < energies:
                target = slab * energies + other
            else:
                target = (slab ^ 1) % slabs * energies + energy
            pairs.append((slab * energies + energy, target))
    return lax.ppermute(x, ("slab", "energy"), pairs)


def in_pair(energy):
    return energy ^ 1


def in_one(energy):
    return energy ^ 2


def in_two(energy):
    return energy + 2 if energy // 2 % 2 == 1 else energy - 2


def per_device(
    onsite,
    hopping,
    separator_hamiltonian,
    coupling,
    bound_rows,
    old_sigma,
    phonon_vertex,
    mode_steps,
    mode_weights,
):
    size, few = hopping.shape[-1], coupling.shape[-1]
    energies, slabs = lax.axis_size("energy"), lax.axis_size("slab")
    assert energies % 2 == 0 and slabs & (slabs - 1) == 0
    half = size // 2
    cube = 3 * 8 * size**3
    full = held(size, 2 * size)
    sigma = old_sigma.reshape(2, size, size)
    given = [
        pltpu.with_memory_space_constraint(x, pltpu.HBM)
        for x in (onsite, hopping[0], sigma, coupling, bound_rows)
    ]
    first, second, start, rows, term = call(
        bound_kernel,
        [full, full, held(size, 2), held(few, 2 * size), held(few, 2 * few)],
        given,
        flops=2 * cube,
        in_specs=[pl.BlockSpec(memory_space=pltpu.HBM)] * len(given),
        scratch_shapes=[pltpu.VMEM(x.shape, x.dtype) for x in given]
        + [pltpu.SemaphoreType.DMA((len(given),))],
    )
    partial, fourth = call(power_kernel, [full, full], [first, second, start], flops=2 * cube)
    near, far, reach = term, None, slabs // 2
    while reach:
        if far is not None:
            far, fourth = lax.optimization_barrier((far, fourth))
            near = near + far
        far = lax.ppermute(near, "slab", [(i, i ^ reach) for i in range(slabs)])
        reach //= 2
    inverse = call(slab_kernel, full, [partial, fourth], flops=cube)
    part = held(half, size)
    middle, *greens = call(
        green_kernel,
        [held(size, 2 * few), part, part],
        [separator_hamiltonian, coupling, bound_rows, inverse, rows, near, far],
        flops=cube,
    )
    parts = []
    for at in (0, 1):
        green_a, green_b = greens
        two_a = exchange(green_a, in_two)
        one_a = exchange(green_a, in_one)
        pair_b = exchange(green_b, in_pair)
        parts.append((green_a, green_b, one_a, two_a, pair_b))
        if at == 0:
            greens = call(imaginary_kernel, [part, part], [middle, rows, inverse], flops=cube // 4)
    combined = []
    for part in parts:
        across_a, one_b, two_b = call(
            combine_kernel, [held(half, size)] * 3, [mode_steps, mode_weights, *part], scalars=2
        )
        two_b = exchange(two_b, in_two)
        one_b = exchange(one_b, in_one)
        across_a = exchange(across_a, in_pair)
        combined.append((across_a, one_b, two_b))
    left = call(
        vertex_left_kernel, jax.ShapeDtypeStruct((size, 3 * size), BF16), [phonon_vertex[0]]
    )
    right = call(
        vertex_right_kernel, jax.ShapeDtypeStruct((3 * size, size), BF16), [phonon_vertex[0]]
    )
    out = None
    for at, (part, more) in enumerate(zip(parts, combined)):
        _, _, one_a, two_a, pair_b = part
        across_a, one_b, two_b = more
        args = [mode_steps, mode_weights, left, right, one_a, two_a, across_a, one_b, two_b, pair_b]
        vmem = pl.BlockSpec(memory_space=pltpu.VMEM)
        specs = [pl.BlockSpec(memory_space=pltpu.SMEM)] * 2 + [vmem] * (len(args) - 2)
        aliases = {}
        if out is not None:
            aliases = {len(args): 0}
            args, specs = [*args, out], [*specs, pl.BlockSpec(memory_space=pl.ANY)]
        out = call(
            functools.partial(dress_kernel, at),
            held(2, size, size),
            args,
            flops=cube // 4,
            in_specs=specs,
            out_specs=pl.BlockSpec(memory_space=pl.ANY),
            scratch_shapes=[pltpu.VMEM((size, size), F32), pltpu.SemaphoreType.DMA((2,))],
            input_output_aliases=aliases,
        )
    return out.reshape(old_sigma.shape)


def solution(mesh):
    placed = (
        P("slab", None),
        P("slab", None, None),
        P(),
        P("slab", None),
        P("slab", None),
        P(None, "energy", "slab", None, None),
        P("slab", None, None),
        P(),
        P(),
    )

    return jax.shard_map(
        per_device,
        mesh=mesh,
        in_specs=placed,
        out_specs=P(None, "energy", "slab", None, None),
        check_vma=False,
    )
```

```python
import functools

import jax
import jax.numpy as jnp
from jax import lax
from jax.experimental import pallas as pl
from jax.experimental.pallas import tpu as pltpu
from jax.sharding import PartitionSpec as P


BROADENING = 1.0
LOWEST = -2.0
SPREAD = 4.0

F32 = jnp.float32
BF16 = jnp.bfloat16
VMEM_BYTES = 24 << 20


def split(x):
    high = x.astype(BF16)
    return high, (x - high.astype(F32)).astype(BF16)


def turned(x):
    half = x.shape[1] // 2
    return jnp.concatenate([-x[:, half:], x[:, :half]], axis=1)


def left_of(x):
    high, low = split(x)
    return jnp.concatenate([high, high, low], axis=1)


def right_of(x):
    high, low = split(x)
    high = jnp.concatenate([high, turned(high)], axis=0)
    low = jnp.concatenate([low, turned(low)], axis=0)
    return jnp.concatenate([high, low, high], axis=0)


def dot(a, b):
    return jnp.dot(a, b, preferred_element_type=F32)


def product(a, b):
    return dot(left_of(a), right_of(b))


def row_scaled(factor, x):
    half = x.shape[1] // 2
    real, imag = x[:, :half], x[:, half:]
    return jnp.concatenate(
        [factor[0] * real - factor[1] * imag, factor[0] * imag + factor[1] * real], axis=1
    )


def same_place(shape):
    rows = lax.broadcasted_iota(jnp.int32, shape, 0)
    cols = lax.broadcasted_iota(jnp.int32, shape, 1)
    return rows == cols


def reciprocal(real, imag):
    magnitude = real * real + imag * imag
    return real / magnitude, -imag / magnitude


def reciprocal_diagonal(real, imag):
    tile = 128
    ways = ([], [])
    for at in range(0, real.shape[0], tile):
        blocks = [x[at : at + tile, at : at + tile] for x in (real, imag)]
        diagonal = same_place(blocks[0].shape)
        blocks = [jnp.where(diagonal, x, jnp.zeros_like(x)) for x in blocks]
        for axis in (0, 1):
            ways[axis].append([jnp.sum(x, axis=axis, keepdims=True) for x in blocks])
    across = [jnp.concatenate(part, axis=1) for part in zip(*ways[0])]
    down = [jnp.concatenate(part, axis=0) for part in zip(*ways[1])]
    return reciprocal(*across), reciprocal(*down)


def remainder(real, imag, across):
    diagonal = same_place(real.shape)
    zero = jnp.zeros_like(real)
    return jnp.concatenate(
        [
            jnp.where(diagonal, zero, imag * across[1] - real * across[0]),
            jnp.where(diagonal, zero, -(real * across[1]) - imag * across[0]),
        ],
        axis=1,
    )


def unit(shape):
    return jnp.where(same_place(shape), 1.0, 0.0)


def energy_here():
    index = lax.axis_index("energy")
    return LOWEST + SPREAD * (index.astype(F32) + 0.5) / lax.axis_size("energy")


def upright(x):
    size = x.shape[1]
    wide = jnp.broadcast_to(x, (size, size))
    return jnp.sum(jnp.where(same_place(wide.shape), wide, jnp.zeros_like(wide)), axis=1, keepdims=True)


def bound_kernel(*refs):
    sources, outs = refs[:5], refs[5:10]
    onsite, hopping, sigma, coupling, bound = places = refs[10:15]
    first_out, second_out, start_out, rows, term = outs
    arrived = refs[15]
    copies = [
        pltpu.make_async_copy(source, target, arrived.at[at])
        for at, (source, target) in enumerate(zip(sources, places))
    ]
    for copy in copies:
        copy.start()
    for copy in copies:
        copy.wait()
    size, few = hopping.shape[0], coupling.shape[1]
    diagonal = same_place(hopping.shape)
    level = energy_here() - onsite[...]
    real = jnp.where(diagonal, level, 0.0) - hopping[...] - sigma[0]
    imag = jnp.where(diagonal, BROADENING, 0.0) - sigma[1]
    across, down = reciprocal_diagonal(real, imag)
    first = remainder(real, imag, across)
    first_out[...] = first
    start_out[...] = jnp.concatenate(down, axis=1)
    second = product(first, first)
    second_out[...] = second
    places = bound[...]
    pick_rows = (
        lax.broadcasted_iota(jnp.int32, (few, size), 1) == upright(places.astype(F32)).astype(jnp.int32)
    ).astype(F32).astype(BF16)
    pick_cols = (lax.broadcasted_iota(jnp.int32, (size, few), 0) == places).astype(F32).astype(BF16)
    strength = coupling[...]
    high, low = split(row_scaled(down, unit(first.shape) + first))
    some = dot(pick_rows, high) + dot(pick_rows, low)
    right = right_of(second)
    some = some + dot(left_of(some), right)
    some = some + dot(left_of(dot(left_of(some), right)), right)
    some = some * upright(strength)
    rows[...] = some
    high, low = split(jnp.concatenate([some[:, :size], some[:, size:]], axis=0))
    corner = dot(high, pick_cols) + dot(low, pick_cols)
    corner = corner * strength
    term[...] = jnp.concatenate([corner[:few], corner[few:]], axis=1)


def power_kernel(first, second, start, partial, fourth):
    size = first.shape[0]
    one, two = first[...], second[...]
    both = dot(jnp.concatenate([left_of(one), left_of(two)], axis=0), right_of(two))
    total = unit(one.shape) + one + two + both[:size]
    partial[...] = row_scaled((start[:, 0:1], start[:, 1:2]), total)
    fourth[...] = both[size:]


def slab_kernel(partial, fourth, inverse):
    inverse[...] = partial[...] + product(partial[...], fourth[...])


def columns_of(x, places):
    size = x.shape[1] // 2
    pick = lax.broadcasted_iota(jnp.int32, (size, places.shape[1]), 0) == places
    pick = pick.astype(F32).astype(BF16)
    high, low = split(jnp.concatenate([x[:, :size], x[:, size:]], axis=0))
    chosen = dot(jnp.concatenate([high, low], axis=1), jnp.concatenate([pick, pick], axis=0))
    return jnp.concatenate([chosen[: x.shape[0]], chosen[x.shape[0] :]], axis=1)


def green_kernel(hamiltonian, coupling, bound, inverse, rows, near, far, middle, green_a, green_b):
    few = hamiltonian.shape[0]
    strength = coupling[...]
    columns = columns_of(inverse[...], bound[...]) * jnp.concatenate([strength, strength], axis=1)
    schur = near[...] + far[...]
    diagonal = same_place(hamiltonian.shape)
    real = jnp.where(diagonal, energy_here(), 0.0) - hamiltonian[...] - schur[:, :few]
    imag = jnp.where(diagonal, BROADENING, 0.0) - schur[:, few:]
    across, down = reciprocal_diagonal(real, imag)
    first = remainder(real, imag, across)
    second = product(first, first)
    both = dot(jnp.concatenate([left_of(first), left_of(second)], axis=0), right_of(second))
    total = row_scaled(down, unit(first.shape) + first + second + both[:few])
    separator = total + product(total, both[few:])
    inner = product(columns, separator)
    middle[...] = inner
    half, size = green_a.shape
    green = inverse[:, :size] + dot(left_of(inner), right_of(rows[...])[:, :size])
    green_a[...] = green[:half]
    green_b[...] = green[half:]


def imaginary_kernel(middle, rows, inverse, green_a, green_b):
    half, size = green_a.shape
    green = inverse[:, size:] + dot(left_of(middle[...]), right_of(rows[...])[:, size:])
    green_a[...] = green[:half]
    green_b[...] = green[half:]


def strengths(steps, weights):
    absorb, emit = [], []
    for distance in (1, 2):
        for row, out in ((0, absorb), (1, emit)):
            total = jnp.zeros((1, 1), F32)
            for mode in range(steps.shape[1]):
                at = slice(mode, mode + 1)
                total = total + jnp.where(steps[:, at] == distance, weights[row : row + 1, at], 0.0)
            out.append(total)
    return absorb, emit


def place():
    energy, count = lax.axis_index("energy"), lax.axis_size("energy")
    odd = lax.rem(energy, 2) == 1
    odd_pair = lax.rem(lax.div(energy, 2), 2) == 1
    lower, higher = energy >= 2, energy + 2 < count
    one = jnp.where(odd_pair, lower.astype(jnp.int32), higher.astype(jnp.int32)) == 1
    two = jnp.where(odd_pair, higher.astype(jnp.int32), lower.astype(jnp.int32)) == 1
    return odd, odd_pair, one, two


def kept(there, x):
    return jnp.where(there, x, jnp.zeros_like(x))


def combine_kernel(steps, weights, green_a, green_b, one_a, two_a, pair_b, across_a, one_b, two_b):
    absorb, emit = strengths(steps, weights)
    odd, odd_pair, one, two = place()
    zero = jnp.zeros((1, 1), F32)
    from_one = jnp.where(odd, jnp.where(odd_pair, absorb[0], zero), jnp.where(odd_pair, zero, emit[0]))
    from_two = jnp.where(odd, jnp.where(odd_pair, zero, absorb[0]), jnp.where(odd_pair, emit[0], zero))
    across_a[...] = (
        jnp.where(odd, emit[0], absorb[0]) * green_a[...]
        + from_one * kept(one, one_a[...])
        + from_two * kept(two, two_a[...])
    )
    up = (absorb[1], jnp.where(odd, zero, absorb[0]))
    down = (emit[1], jnp.where(odd, emit[0], zero))
    for out, first, second in ((one_b, up, down), (two_b, down, up)):
        own, other = [jnp.where(odd_pair, b, a) for a, b in zip(first, second)]
        out[...] = own * green_b[...] + other * pair_b[...]


def dress_kernel(at, steps, weights, left, right, one_a, two_a, across_a, one_b, two_b, pair_b, *rest):
    out, held_out, sent = rest[-3:]
    absorb, emit = strengths(steps, weights)
    odd, odd_pair, one, two = place()
    from_one = jnp.where(odd_pair, absorb[1], emit[1])
    from_two = jnp.where(odd_pair, emit[1], absorb[1])
    mixed_a = from_one * kept(one, one_a[...]) + from_two * kept(two, two_a[...]) + across_a[...]
    mixed_b = (
        kept(one, one_b[...]) + kept(two, two_b[...]) + jnp.where(odd, absorb[0], emit[0]) * pair_b[...]
    )
    high, low = split(jnp.concatenate([mixed_a, mixed_b], axis=0))
    high, low = split(dot(left[...], jnp.concatenate([high, low, high], axis=0)))
    outer = jnp.concatenate([high, high, low], axis=1)
    half = mixed_a.shape[0]
    copies = []
    for piece in (0, 1):
        rows = pl.ds(piece * half, half)
        held_out[rows] = dot(outer[piece * half : piece * half + half], right[...])
        copies.append(pltpu.make_async_copy(held_out.at[rows], out.at[at, rows], sent.at[piece]))
        copies[-1].start()
    for copy in copies:
        copy.wait()


def vertex_left_kernel(vertex, left):
    high, low = split(vertex[...])
    left[...] = jnp.concatenate([high, high, low], axis=1)


def vertex_right_kernel(vertex, right):
    size = vertex.shape[0]
    high, low = split(vertex[...].T)
    for at, part in enumerate((high, low, high)):
        right[at * size : (at + 1) * size, :] = part


def call(kernel, outs, args, flops=0, **kept):
    vmem = pl.BlockSpec(memory_space=pltpu.VMEM)
    touched = sum(4 * a.size for a in [*args, *jax.tree.leaves(outs)])
    settings = dict(
        in_specs=[vmem] * len(args),
        out_specs=jax.tree.map(lambda _: vmem, outs),
    )
    settings.update(kept)
    return pl.pallas_call(
        kernel,
        out_shape=outs,
        compiler_params=pltpu.CompilerParams(vmem_limit_bytes=VMEM_BYTES),
        cost_estimate=pl.CostEstimate(flops=flops, bytes_accessed=touched, transcendentals=0),
        **settings,
    )(*args)


def held(*shape):
    return jax.ShapeDtypeStruct(shape, F32)


def exchange(x, partner):
    slabs, energies = lax.axis_size("slab"), lax.axis_size("energy")
    pairs = []
    for slab in range(slabs):
        for energy in range(energies):
            other = partner(energy)
            if 0 <= other < energies:
                target = slab * energies + other
            else:
                target = (slab ^ 1) % slabs * energies + energy
            pairs.append((slab * energies + energy, target))
    return lax.ppermute(x, ("slab", "energy"), pairs)


def in_pair(energy):
    return energy ^ 1


def in_one(energy):
    return energy ^ 2


def in_two(energy):
    return energy + 2 if energy // 2 % 2 == 1 else energy - 2


def per_device(
    onsite,
    hopping,
    separator_hamiltonian,
    coupling,
    bound_rows,
    old_sigma,
    phonon_vertex,
    mode_steps,
    mode_weights,
):
    size, few = hopping.shape[-1], coupling.shape[-1]
    energies, slabs = lax.axis_size("energy"), lax.axis_size("slab")
    assert energies % 2 == 0 and slabs & (slabs - 1) == 0
    half = size // 2
    cube = 3 * 8 * size**3
    full = held(size, 2 * size)
    sigma = old_sigma.reshape(2, size, size)
    mode_steps = mode_steps[None]
    given = [
        pltpu.with_memory_space_constraint(x, pltpu.HBM)
        for x in (onsite, hopping[0], sigma, coupling, bound_rows)
    ]
    first, second, start, rows, term = call(
        bound_kernel,
        [full, full, held(size, 2), held(few, 2 * size), held(few, 2 * few)],
        given,
        flops=2 * cube,
        in_specs=[pl.BlockSpec(memory_space=pltpu.HBM)] * len(given),
        scratch_shapes=[pltpu.VMEM(x.shape, x.dtype) for x in given]
        + [pltpu.SemaphoreType.DMA((len(given),))],
    )
    partial, fourth = call(power_kernel, [full, full], [first, second, start], flops=2 * cube)
    near, far, reach = term, None, slabs // 2
    while reach:
        if far is not None:
            far, fourth = lax.optimization_barrier((far, fourth))
            near = near + far
        far = lax.ppermute(near, "slab", [(i, i ^ reach) for i in range(slabs)])
        reach //= 2
    inverse = call(slab_kernel, full, [partial, fourth], flops=cube)
    part = held(half, size)
    middle, *greens = call(
        green_kernel,
        [held(size, 2 * few), part, part],
        [separator_hamiltonian, coupling, bound_rows, inverse, rows, near, far],
        flops=cube,
    )
    parts = []
    for at in (0, 1):
        green_a, green_b = greens
        two_a = exchange(green_a, in_two)
        one_a = exchange(green_a, in_one)
        pair_b = exchange(green_b, in_pair)
        parts.append((green_a, green_b, one_a, two_a, pair_b))
        if at == 0:
            greens = call(imaginary_kernel, [part, part], [middle, rows, inverse], flops=cube // 4)
    combined = []
    for part in parts:
        across_a, one_b, two_b = call(
            combine_kernel, [held(half, size)] * 3, [mode_steps, mode_weights, *part]
        )
        two_b = exchange(two_b, in_two)
        one_b = exchange(one_b, in_one)
        across_a = exchange(across_a, in_pair)
        combined.append((across_a, one_b, two_b))
    left = call(
        vertex_left_kernel, jax.ShapeDtypeStruct((size, 3 * size), BF16), [phonon_vertex[0]]
    )
    right = call(
        vertex_right_kernel, jax.ShapeDtypeStruct((3 * size, size), BF16), [phonon_vertex[0]]
    )
    out = None
    for at, (part, more) in enumerate(zip(parts, combined)):
        _, _, one_a, two_a, pair_b = part
        across_a, one_b, two_b = more
        args = [mode_steps, mode_weights, left, right, one_a, two_a, across_a, one_b, two_b, pair_b]
        vmem = pl.BlockSpec(memory_space=pltpu.VMEM)
        specs = [vmem] * len(args)
        aliases = {}
        if out is not None:
            aliases = {len(args): 0}
            args, specs = [*args, out], [*specs, pl.BlockSpec(memory_space=pl.ANY)]
        out = call(
            functools.partial(dress_kernel, at),
            held(2, size, size),
            args,
            flops=cube // 4,
            in_specs=specs,
            out_specs=pl.BlockSpec(memory_space=pl.ANY),
            scratch_shapes=[pltpu.VMEM((size, size), F32), pltpu.SemaphoreType.DMA((2,))],
            input_output_aliases=aliases,
        )
    return out.reshape(old_sigma.shape)


def solution(mesh):
    placed = (
        P("slab", None),
        P("slab", None, None),
        P(),
        P("slab", None),
        P("slab", None),
        P(None, "energy", "slab", None, None),
        P("slab", None, None),
        P(),
        P(),
    )

    return jax.shard_map(
        per_device,
        mesh=mesh,
        in_specs=placed,
        out_specs=P(None, "energy", "slab", None, None),
        check_vma=False,
    )
```

```python
import functools

import jax
import jax.numpy as jnp
from jax import lax
from jax.experimental import pallas as pl
from jax.experimental.pallas import tpu as pltpu
from jax.sharding import PartitionSpec as P


BROADENING = 1.0
LOWEST = -2.0
SPREAD = 4.0

F32 = jnp.float32
BF16 = jnp.bfloat16
VMEM_BYTES = 24 << 20


def split(x):
    high = x.astype(BF16)
    return high, (x - high.astype(F32)).astype(BF16)


def turned(x):
    half = x.shape[1] // 2
    return jnp.concatenate([-x[:, half:], x[:, :half]], axis=1)


def left_of(x):
    high, low = split(x)
    return jnp.concatenate([high, high, low], axis=1)


def right_of(x):
    high, low = split(x)
    high = jnp.concatenate([high, turned(high)], axis=0)
    low = jnp.concatenate([low, turned(low)], axis=0)
    return jnp.concatenate([high, low, high], axis=0)


def dot(a, b):
    return jnp.dot(a, b, preferred_element_type=F32)


def product(a, b):
    return dot(left_of(a), right_of(b))


def row_scaled(factor, x):
    half = x.shape[1] // 2
    real, imag = x[:, :half], x[:, half:]
    return jnp.concatenate(
        [factor[0] * real - factor[1] * imag, factor[0] * imag + factor[1] * real], axis=1
    )


def same_place(shape):
    rows = lax.broadcasted_iota(jnp.int32, shape, 0)
    cols = lax.broadcasted_iota(jnp.int32, shape, 1)
    return rows == cols


def reciprocal(real, imag):
    magnitude = real * real + imag * imag
    return real / magnitude, -imag / magnitude


def reciprocal_diagonal(real, imag):
    tile = 128
    ways = ([], [])
    for at in range(0, real.shape[0], tile):
        blocks = [x[at : at + tile, at : at + tile] for x in (real, imag)]
        diagonal = same_place(blocks[0].shape)
        blocks = [jnp.where(diagonal, x, jnp.zeros_like(x)) for x in blocks]
        for axis in (0, 1):
            ways[axis].append([jnp.sum(x, axis=axis, keepdims=True) for x in blocks])
    across = [jnp.concatenate(part, axis=1) for part in zip(*ways[0])]
    down = [jnp.concatenate(part, axis=0) for part in zip(*ways[1])]
    return reciprocal(*across), reciprocal(*down)


def remainder(real, imag, across):
    diagonal = same_place(real.shape)
    zero = jnp.zeros_like(real)
    return jnp.concatenate(
        [
            jnp.where(diagonal, zero, imag * across[1] - real * across[0]),
            jnp.where(diagonal, zero, -(real * across[1]) - imag * across[0]),
        ],
        axis=1,
    )


def unit(shape):
    return jnp.where(same_place(shape), 1.0, 0.0)


def energy_here():
    index = lax.axis_index("energy")
    return LOWEST + SPREAD * (index.astype(F32) + 0.5) / lax.axis_size("energy")


def upright(x):
    size = x.shape[1]
    wide = jnp.broadcast_to(x, (size, size))
    return jnp.sum(jnp.where(same_place(wide.shape), wide, jnp.zeros_like(wide)), axis=1, keepdims=True)


def bound_kernel(*refs):
    sources, outs = refs[:5], refs[5:10]
    onsite, hopping, sigma, coupling, bound = places = refs[10:15]
    first_out, second_out, start_out, rows, term = outs
    arrived = refs[15]
    copies = [
        pltpu.make_async_copy(source, target, arrived.at[at])
        for at, (source, target) in enumerate(zip(sources, places))
    ]
    for at in (2, 1, 0, 4, 3):
        copies[at].start()
    for copy in copies:
        copy.wait()
    size, few = hopping.shape[0], coupling.shape[1]
    diagonal = same_place(hopping.shape)
    level = energy_here() - onsite[...]
    real = jnp.where(diagonal, level, 0.0) - hopping[...] - sigma[0]
    imag = jnp.where(diagonal, BROADENING, 0.0) - sigma[1]
    across, down = reciprocal_diagonal(real, imag)
    first = remainder(real, imag, across)
    first_out[...] = first
    start_out[...] = jnp.concatenate(down, axis=1)
    second = product(first, first)
    second_out[...] = second
    places = bound[...]
    pick_rows = (
        lax.broadcasted_iota(jnp.int32, (few, size), 1) == upright(places.astype(F32)).astype(jnp.int32)
    ).astype(F32).astype(BF16)
    pick_cols = (lax.broadcasted_iota(jnp.int32, (size, few), 0) == places).astype(F32).astype(BF16)
    strength = coupling[...]
    high, low = split(row_scaled(down, unit(first.shape) + first))
    some = dot(pick_rows, high) + dot(pick_rows, low)
    right = right_of(second)
    some = some + dot(left_of(some), right)
    some = some + dot(left_of(dot(left_of(some), right)), right)
    some = some * upright(strength)
    rows[...] = some
    high, low = split(jnp.concatenate([some[:, :size], some[:, size:]], axis=0))
    corner = dot(high, pick_cols) + dot(low, pick_cols)
    corner = corner * strength
    term[...] = jnp.concatenate([corner[:few], corner[few:]], axis=1)


def power_kernel(first, second, start, partial, left, right):
    size = first.shape[0]
    one, two = first[...], second[...]
    both = dot(jnp.concatenate([left_of(one), left_of(two)], axis=0), right_of(two))
    total = unit(one.shape) + one + two + both[:size]
    total = row_scaled((start[:, 0:1], start[:, 1:2]), total)
    partial[...] = total
    left[...] = jnp.concatenate(split(total), axis=1)
    high, low = split(both[size:])
    for at, part in enumerate((high, turned(high), low, turned(low))):
        right[at * size : (at + 1) * size] = part


def slab_kernel(partial, left, right, inverse):
    wide = partial.shape[1]
    high, low = left[:, :wide], left[:, wide:]
    inverse[...] = partial[...] + dot(
        jnp.concatenate([high, high, low], axis=1),
        jnp.concatenate([right[...], right[:wide]], axis=0),
    )


def columns_of(x, places):
    size = x.shape[1] // 2
    pick = lax.broadcasted_iota(jnp.int32, (size, places.shape[1]), 0) == places
    pick = pick.astype(F32).astype(BF16)
    high, low = split(jnp.concatenate([x[:, :size], x[:, size:]], axis=0))
    chosen = dot(jnp.concatenate([high, low], axis=1), jnp.concatenate([pick, pick], axis=0))
    return jnp.concatenate([chosen[: x.shape[0]], chosen[x.shape[0] :]], axis=1)


def green_kernel(hamiltonian, coupling, bound, inverse, rows, near, far, middle, green_a, green_b):
    few = hamiltonian.shape[0]
    strength = coupling[...]
    columns = columns_of(inverse[...], bound[...]) * jnp.concatenate([strength, strength], axis=1)
    schur = near[...] + far[...]
    diagonal = same_place(hamiltonian.shape)
    real = jnp.where(diagonal, energy_here(), 0.0) - hamiltonian[...] - schur[:, :few]
    imag = jnp.where(diagonal, BROADENING, 0.0) - schur[:, few:]
    across, down = reciprocal_diagonal(real, imag)
    first = remainder(real, imag, across)
    second = product(first, first)
    both = dot(jnp.concatenate([left_of(first), left_of(second)], axis=0), right_of(second))
    total = row_scaled(down, unit(first.shape) + first + second + both[:few])
    separator = total + product(total, both[few:])
    inner = product(columns, separator)
    middle[...] = inner
    half, size = green_a.shape
    green = inverse[:, :size] + dot(left_of(inner), right_of(rows[...])[:, :size])
    green_a[...] = green[:half]
    green_b[...] = green[half:]


def imaginary_kernel(middle, rows, inverse, green_a, green_b):
    half, size = green_a.shape
    green = inverse[:, size:] + dot(left_of(middle[...]), right_of(rows[...])[:, size:])
    green_a[...] = green[:half]
    green_b[...] = green[half:]


def strengths(steps, weights):
    absorb, emit = [], []
    for distance in (1, 2):
        for row, out in ((0, absorb), (1, emit)):
            total = jnp.zeros((1, 1), F32)
            for mode in range(steps.shape[1]):
                at = slice(mode, mode + 1)
                total = total + jnp.where(steps[:, at] == distance, weights[row : row + 1, at], 0.0)
            out.append(total)
    return absorb, emit


def place():
    energy, count = lax.axis_index("energy"), lax.axis_size("energy")
    odd = lax.rem(energy, 2) == 1
    odd_pair = lax.rem(lax.div(energy, 2), 2) == 1
    lower, higher = energy >= 2, energy + 2 < count
    one = jnp.where(odd_pair, lower.astype(jnp.int32), higher.astype(jnp.int32)) == 1
    two = jnp.where(odd_pair, higher.astype(jnp.int32), lower.astype(jnp.int32)) == 1
    return odd, odd_pair, one, two


def kept(there, x):
    return jnp.where(there, x, jnp.zeros_like(x))


def combine_kernel(steps, weights, green_a, green_b, one_a, two_a, pair_b, across_a, one_b, two_b):
    absorb, emit = strengths(steps, weights)
    odd, odd_pair, one, two = place()
    zero = jnp.zeros((1, 1), F32)
    from_one = jnp.where(odd, jnp.where(odd_pair, absorb[0], zero), jnp.where(odd_pair, zero, emit[0]))
    from_two = jnp.where(odd, jnp.where(odd_pair, zero, absorb[0]), jnp.where(odd_pair, emit[0], zero))
    across_a[...] = (
        jnp.where(odd, emit[0], absorb[0]) * green_a[...]
        + from_one * kept(one, one_a[...])
        + from_two * kept(two, two_a[...])
    )
    up = (absorb[1], jnp.where(odd, zero, absorb[0]))
    down = (emit[1], jnp.where(odd, emit[0], zero))
    for out, first, second in ((one_b, up, down), (two_b, down, up)):
        own, other = [jnp.where(odd_pair, b, a) for a, b in zip(first, second)]
        out[...] = own * green_b[...] + other * pair_b[...]


def dress_kernel(at, steps, weights, left, right, one_a, two_a, across_a, one_b, two_b, pair_b, *rest):
    out, held_out, sent = rest[-3:]
    absorb, emit = strengths(steps, weights)
    odd, odd_pair, one, two = place()
    from_one = jnp.where(odd_pair, absorb[1], emit[1])
    from_two = jnp.where(odd_pair, emit[1], absorb[1])
    mixed_a = from_one * kept(one, one_a[...]) + from_two * kept(two, two_a[...]) + across_a[...]
    mixed_b = (
        kept(one, one_b[...]) + kept(two, two_b[...]) + jnp.where(odd, absorb[0], emit[0]) * pair_b[...]
    )
    high, low = split(jnp.concatenate([mixed_a, mixed_b], axis=0))
    high, low = split(dot(left[...], jnp.concatenate([high, low, high], axis=0)))
    outer = jnp.concatenate([high, high, low], axis=1)
    half = mixed_a.shape[0]
    copies = []
    for piece in (0, 1):
        rows = pl.ds(piece * half, half)
        held_out[rows] = dot(outer[piece * half : piece * half + half], right[...])
        copies.append(pltpu.make_async_copy(held_out.at[rows], out.at[at, rows], sent.at[piece]))
        copies[-1].start()
    for copy in copies:
        copy.wait()


def vertex_left_kernel(vertex, left):
    high, low = split(vertex[...])
    left[...] = jnp.concatenate([high, high, low], axis=1)


def vertex_right_kernel(vertex, right):
    size = vertex.shape[0]
    high, low = split(vertex[...].T)
    for at, part in enumerate((high, low, high)):
        right[at * size : (at + 1) * size, :] = part


def call(kernel, outs, args, flops=0, **kept):
    vmem = pl.BlockSpec(memory_space=pltpu.VMEM)
    touched = sum(4 * a.size for a in [*args, *jax.tree.leaves(outs)])
    settings = dict(
        in_specs=[vmem] * len(args),
        out_specs=jax.tree.map(lambda _: vmem, outs),
    )
    settings.update(kept)
    return pl.pallas_call(
        kernel,
        out_shape=outs,
        compiler_params=pltpu.CompilerParams(vmem_limit_bytes=VMEM_BYTES),
        cost_estimate=pl.CostEstimate(flops=flops, bytes_accessed=touched, transcendentals=0),
        **settings,
    )(*args)


def held(*shape):
    return jax.ShapeDtypeStruct(shape, F32)


def exchange(x, partner):
    slabs, energies = lax.axis_size("slab"), lax.axis_size("energy")
    pairs = []
    for slab in range(slabs):
        for energy in range(energies):
            other = partner(energy)
            if 0 <= other < energies:
                target = slab * energies + other
            else:
                target = (slab ^ 1) % slabs * energies + energy
            pairs.append((slab * energies + energy, target))
    return lax.ppermute(x, ("slab", "energy"), pairs)


def in_pair(energy):
    return energy ^ 1


def in_one(energy):
    return energy ^ 2


def in_two(energy):
    return energy + 2 if energy // 2 % 2 == 1 else energy - 2


def per_device(
    onsite,
    hopping,
    separator_hamiltonian,
    coupling,
    bound_rows,
    old_sigma,
    phonon_vertex,
    mode_steps,
    mode_weights,
):
    size, few = hopping.shape[-1], coupling.shape[-1]
    energies, slabs = lax.axis_size("energy"), lax.axis_size("slab")
    assert energies % 2 == 0 and slabs & (slabs - 1) == 0
    half = size // 2
    cube = 3 * 8 * size**3
    full = held(size, 2 * size)
    sigma = old_sigma.reshape(2, size, size)
    mode_steps = mode_steps[None]
    given = [
        pltpu.with_memory_space_constraint(x, pltpu.HBM)
        for x in (onsite, hopping[0], sigma, coupling, bound_rows)
    ]
    first, second, start, rows, term = call(
        bound_kernel,
        [full, full, held(size, 2), held(few, 2 * size), held(few, 2 * few)],
        given,
        flops=2 * cube,
        in_specs=[pl.BlockSpec(memory_space=pltpu.HBM)] * len(given),
        scratch_shapes=[pltpu.VMEM(x.shape, x.dtype) for x in given]
        + [pltpu.SemaphoreType.DMA((len(given),))],
    )
    partial, left_side, right_side = call(
        power_kernel,
        [
            full,
            jax.ShapeDtypeStruct((size, 4 * size), BF16),
            jax.ShapeDtypeStruct((4 * size, 2 * size), BF16),
        ],
        [first, second, start],
        flops=2 * cube,
    )
    near, far, reach = term, None, slabs // 2
    while reach:
        if far is not None:
            far, partial = lax.optimization_barrier((far, partial))
            near = near + far
        far = lax.ppermute(near, "slab", [(i, i ^ reach) for i in range(slabs)])
        reach //= 2
    inverse = call(slab_kernel, full, [partial, left_side, right_side], flops=cube)
    part = held(half, size)
    middle, *greens = call(
        green_kernel,
        [held(size, 2 * few), part, part],
        [separator_hamiltonian, coupling, bound_rows, inverse, rows, near, far],
        flops=cube,
    )
    parts = []
    for at in (0, 1):
        green_a, green_b = greens
        two_a = exchange(green_a, in_two)
        one_a = exchange(green_a, in_one)
        pair_b = exchange(green_b, in_pair)
        parts.append((green_a, green_b, one_a, two_a, pair_b))
        if at == 0:
            greens = call(imaginary_kernel, [part, part], [middle, rows, inverse], flops=cube // 4)
    combined = []
    for part in parts:
        across_a, one_b, two_b = call(
            combine_kernel, [held(half, size)] * 3, [mode_steps, mode_weights, *part]
        )
        two_b = exchange(two_b, in_two)
        one_b = exchange(one_b, in_one)
        across_a = exchange(across_a, in_pair)
        combined.append((across_a, one_b, two_b))
    left = call(
        vertex_left_kernel, jax.ShapeDtypeStruct((size, 3 * size), BF16), [phonon_vertex[0]]
    )
    right = call(
        vertex_right_kernel, jax.ShapeDtypeStruct((3 * size, size), BF16), [phonon_vertex[0]]
    )
    out = None
    for at, (part, more) in enumerate(zip(parts, combined)):
        _, _, one_a, two_a, pair_b = part
        across_a, one_b, two_b = more
        args = [mode_steps, mode_weights, left, right, one_a, two_a, across_a, one_b, two_b, pair_b]
        vmem = pl.BlockSpec(memory_space=pltpu.VMEM)
        specs = [vmem] * len(args)
        aliases = {}
        if out is not None:
            aliases = {len(args): 0}
            args, specs = [*args, out], [*specs, pl.BlockSpec(memory_space=pl.ANY)]
        out = call(
            functools.partial(dress_kernel, at),
            held(2, size, size),
            args,
            flops=cube // 4,
            in_specs=specs,
            out_specs=pl.BlockSpec(memory_space=pl.ANY),
            scratch_shapes=[pltpu.VMEM((size, size), F32), pltpu.SemaphoreType.DMA((2,))],
            input_output_aliases=aliases,
        )
    return out.reshape(old_sigma.shape)


def solution(mesh):
    placed = (
        P("slab", None),
        P("slab", None, None),
        P(),
        P("slab", None),
        P("slab", None),
        P(None, "energy", "slab", None, None),
        P("slab", None, None),
        P(),
        P(),
    )

    return jax.shard_map(
        per_device,
        mesh=mesh,
        in_specs=placed,
        out_specs=P(None, "energy", "slab", None, None),
        check_vma=False,
    )
```

```python
import functools

import jax
import jax.numpy as jnp
from jax import lax
from jax.experimental import pallas as pl
from jax.experimental.pallas import tpu as pltpu
from jax.sharding import PartitionSpec as P


BROADENING = 1.0
LOWEST = -2.0
SPREAD = 4.0

F32 = jnp.float32
BF16 = jnp.bfloat16
VMEM_BYTES = 24 << 20


def split(x):
    high = x.astype(BF16)
    return high, (x - high.astype(F32)).astype(BF16)


def turned(x):
    half = x.shape[1] // 2
    return jnp.concatenate([-x[:, half:], x[:, :half]], axis=1)


def left_of(x):
    high, low = split(x)
    return jnp.concatenate([high, high, low], axis=1)


def right_of(x):
    high, low = split(x)
    high = jnp.concatenate([high, turned(high)], axis=0)
    low = jnp.concatenate([low, turned(low)], axis=0)
    return jnp.concatenate([high, low, high], axis=0)


def dot(a, b):
    return jnp.dot(a, b, preferred_element_type=F32)


def product(a, b):
    return dot(left_of(a), right_of(b))


def row_scaled(factor, x):
    half = x.shape[1] // 2
    real, imag = x[:, :half], x[:, half:]
    return jnp.concatenate(
        [factor[0] * real - factor[1] * imag, factor[0] * imag + factor[1] * real], axis=1
    )


def same_place(shape):
    rows = lax.broadcasted_iota(jnp.int32, shape, 0)
    cols = lax.broadcasted_iota(jnp.int32, shape, 1)
    return rows == cols


def reciprocal(real, imag):
    magnitude = real * real + imag * imag
    return real / magnitude, -imag / magnitude


def reciprocal_diagonal(real, imag):
    tile = 128
    ways = ([], [])
    for at in range(0, real.shape[0], tile):
        blocks = [x[at : at + tile, at : at + tile] for x in (real, imag)]
        diagonal = same_place(blocks[0].shape)
        blocks = [jnp.where(diagonal, x, jnp.zeros_like(x)) for x in blocks]
        for axis in (0, 1):
            ways[axis].append([jnp.sum(x, axis=axis, keepdims=True) for x in blocks])
    across = [jnp.concatenate(part, axis=1) for part in zip(*ways[0])]
    down = [jnp.concatenate(part, axis=0) for part in zip(*ways[1])]
    return reciprocal(*across), reciprocal(*down)


def remainder(real, imag, across):
    diagonal = same_place(real.shape)
    zero = jnp.zeros_like(real)
    return jnp.concatenate(
        [
            jnp.where(diagonal, zero, imag * across[1] - real * across[0]),
            jnp.where(diagonal, zero, -(real * across[1]) - imag * across[0]),
        ],
        axis=1,
    )


def unit(shape):
    return jnp.where(same_place(shape), 1.0, 0.0)


def energy_here():
    index = lax.axis_index("energy")
    return LOWEST + SPREAD * (index.astype(F32) + 0.5) / lax.axis_size("energy")


def upright(x):
    size = x.shape[1]
    wide = jnp.broadcast_to(x, (size, size))
    return jnp.sum(jnp.where(same_place(wide.shape), wide, jnp.zeros_like(wide)), axis=1, keepdims=True)


def bound_kernel(*refs):
    sources, outs = refs[:5], refs[5:10]
    onsite, hopping, sigma, coupling, bound = places = refs[10:15]
    first_out, second_out, start_out, rows, term = outs
    arrived = refs[15]
    copies = [
        pltpu.make_async_copy(source, target, arrived.at[at])
        for at, (source, target) in enumerate(zip(sources, places))
    ]
    for at in (2, 1, 0, 4, 3):
        copies[at].start()
    for copy in copies:
        copy.wait()
    size, few = hopping.shape[0], coupling.shape[1]
    diagonal = same_place(hopping.shape)
    level = energy_here() - onsite[...]
    real = jnp.where(diagonal, level, 0.0) - hopping[...] - sigma[0]
    imag = jnp.where(diagonal, BROADENING, 0.0) - sigma[1]
    across, down = reciprocal_diagonal(real, imag)
    first = remainder(real, imag, across)
    first_out[...] = first
    start_out[...] = jnp.concatenate(down, axis=1)
    second = product(first, first)
    second_out[...] = second
    places = bound[...]
    pick_rows = (
        lax.broadcasted_iota(jnp.int32, (few, size), 1) == upright(places.astype(F32)).astype(jnp.int32)
    ).astype(F32).astype(BF16)
    pick_cols = (lax.broadcasted_iota(jnp.int32, (size, few), 0) == places).astype(F32).astype(BF16)
    strength = coupling[...]
    high, low = split(row_scaled(down, unit(first.shape) + first))
    some = dot(pick_rows, high) + dot(pick_rows, low)
    right = right_of(second)
    some = some + dot(left_of(some), right)
    some = some + dot(left_of(dot(left_of(some), right)), right)
    some = some * upright(strength)
    rows[...] = some
    high, low = split(jnp.concatenate([some[:, :size], some[:, size:]], axis=0))
    corner = dot(high, pick_cols) + dot(low, pick_cols)
    corner = corner * strength
    term[...] = jnp.concatenate([corner[:few], corner[few:]], axis=1)


def power_kernel(first, second, start, partial, left, right):
    size = first.shape[0]
    one, two = first[...], second[...]
    both = dot(jnp.concatenate([left_of(one), left_of(two)], axis=0), right_of(two))
    total = unit(one.shape) + one + two + both[:size]
    total = row_scaled((start[:, 0:1], start[:, 1:2]), total)
    partial[...] = total
    left[...] = jnp.concatenate(split(total), axis=1)
    high, low = split(both[size:])
    for at, part in enumerate((high, turned(high), low, turned(low))):
        right[at * size : (at + 1) * size] = part


def slab_kernel(partial, left, right, inverse):
    wide = partial.shape[1]
    high, low = left[:, :wide], left[:, wide:]
    inverse[...] = partial[...] + dot(
        jnp.concatenate([high, high, low], axis=1),
        jnp.concatenate([right[...], right[:wide]], axis=0),
    )


def columns_of(x, places):
    size = x.shape[1] // 2
    pick = lax.broadcasted_iota(jnp.int32, (size, places.shape[1]), 0) == places
    pick = pick.astype(F32).astype(BF16)
    high, low = split(jnp.concatenate([x[:, :size], x[:, size:]], axis=0))
    chosen = dot(jnp.concatenate([high, low], axis=1), jnp.concatenate([pick, pick], axis=0))
    return jnp.concatenate([chosen[: x.shape[0]], chosen[x.shape[0] :]], axis=1)


def green_kernel(hamiltonian, coupling, bound, inverse, rows, near, far, middle, green_a, green_b):
    few = hamiltonian.shape[0]
    strength = coupling[...]
    columns = columns_of(inverse[...], bound[...]) * jnp.concatenate([strength, strength], axis=1)
    schur = near[...] + far[...]
    diagonal = same_place(hamiltonian.shape)
    real = jnp.where(diagonal, energy_here(), 0.0) - hamiltonian[...] - schur[:, :few]
    imag = jnp.where(diagonal, BROADENING, 0.0) - schur[:, few:]
    across, down = reciprocal_diagonal(real, imag)
    first = remainder(real, imag, across)
    second = product(first, first)
    both = dot(jnp.concatenate([left_of(first), left_of(second)], axis=0), right_of(second))
    total = row_scaled(down, unit(first.shape) + first + second + both[:few])
    separator = total + product(total, both[few:])
    inner = product(columns, separator)
    middle[...] = inner
    half, size = green_a.shape
    green = inverse[:, :size] + dot(left_of(inner), right_of(rows[...])[:, :size])
    green_a[...] = green[:half]
    green_b[...] = green[half:]


def imaginary_kernel(middle, rows, inverse, green_a, green_b):
    half, size = green_a.shape
    green = inverse[:, size:] + dot(left_of(middle[...]), right_of(rows[...])[:, size:])
    green_a[...] = green[:half]
    green_b[...] = green[half:]


def strengths(steps, weights):
    absorb, emit = [], []
    for distance in (1, 2):
        for row, out in ((0, absorb), (1, emit)):
            total = jnp.zeros((1, 1), F32)
            for mode in range(steps.shape[1]):
                at = slice(mode, mode + 1)
                total = total + jnp.where(steps[:, at] == distance, weights[row : row + 1, at], 0.0)
            out.append(total)
    return absorb, emit


def place():
    energy, count = lax.axis_index("energy"), lax.axis_size("energy")
    odd = lax.rem(energy, 2) == 1
    odd_pair = lax.rem(lax.div(energy, 2), 2) == 1
    lower, higher = energy >= 2, energy + 2 < count
    one = jnp.where(odd_pair, lower.astype(jnp.int32), higher.astype(jnp.int32)) == 1
    two = jnp.where(odd_pair, higher.astype(jnp.int32), lower.astype(jnp.int32)) == 1
    return odd, odd_pair, one, two


def kept(there, x):
    return jnp.where(there, x, jnp.zeros_like(x))


def combine_kernel(steps, weights, green_a, green_b, one_a, two_a, pair_b, across_a, one_b, two_b):
    absorb, emit = strengths(steps, weights)
    odd, odd_pair, one, two = place()
    zero = jnp.zeros((1, 1), F32)
    from_one = jnp.where(odd, jnp.where(odd_pair, absorb[0], zero), jnp.where(odd_pair, zero, emit[0]))
    from_two = jnp.where(odd, jnp.where(odd_pair, zero, absorb[0]), jnp.where(odd_pair, emit[0], zero))
    across_a[...] = (
        jnp.where(odd, emit[0], absorb[0]) * green_a[...]
        + from_one * kept(one, one_a[...])
        + from_two * kept(two, two_a[...])
    )
    up = (absorb[1], jnp.where(odd, zero, absorb[0]))
    down = (emit[1], jnp.where(odd, emit[0], zero))
    for out, first, second in ((one_b, up, down), (two_b, down, up)):
        own, other = [jnp.where(odd_pair, b, a) for a, b in zip(first, second)]
        out[...] = own * green_b[...] + other * pair_b[...]


def dress_kernel(at, steps, weights, left, right, one_a, two_a, across_a, one_b, two_b, pair_b, *rest):
    out, held_out, sent = rest[-3:]
    absorb, emit = strengths(steps, weights)
    odd, odd_pair, one, two = place()
    from_one = jnp.where(odd_pair, absorb[1], emit[1])
    from_two = jnp.where(odd_pair, emit[1], absorb[1])
    mixed_a = from_one * kept(one, one_a[...]) + from_two * kept(two, two_a[...]) + across_a[...]
    mixed_b = (
        kept(one, one_b[...]) + kept(two, two_b[...]) + jnp.where(odd, absorb[0], emit[0]) * pair_b[...]
    )
    high, low = split(jnp.concatenate([mixed_a, mixed_b], axis=0))
    high, low = split(dot(left[...], jnp.concatenate([high, low, high], axis=0)))
    outer = jnp.concatenate([high, high, low], axis=1)
    size = left.shape[0]
    cut = size * 2 // 3 // 16 * 16
    copies = []
    for piece, (row, count) in enumerate(((0, cut), (cut, size - cut))):
        rows = pl.ds(row, count)
        held_out[rows] = dot(outer[row : row + count], right[...])
        copies.append(pltpu.make_async_copy(held_out.at[rows], out.at[at, rows], sent.at[piece]))
        copies[-1].start()
    for copy in copies:
        copy.wait()


def vertex_left_kernel(vertex, left):
    high, low = split(vertex[...])
    left[...] = jnp.concatenate([high, high, low], axis=1)


def vertex_right_kernel(vertex, right):
    size = vertex.shape[0]
    high, low = split(vertex[...].T)
    for at, part in enumerate((high, low, high)):
        right[at * size : (at + 1) * size, :] = part


def call(kernel, outs, args, flops=0, **kept):
    vmem = pl.BlockSpec(memory_space=pltpu.VMEM)
    touched = sum(4 * a.size for a in [*args, *jax.tree.leaves(outs)])
    settings = dict(
        in_specs=[vmem] * len(args),
        out_specs=jax.tree.map(lambda _: vmem, outs),
    )
    settings.update(kept)
    return pl.pallas_call(
        kernel,
        out_shape=outs,
        compiler_params=pltpu.CompilerParams(vmem_limit_bytes=VMEM_BYTES),
        cost_estimate=pl.CostEstimate(flops=flops, bytes_accessed=touched, transcendentals=0),
        **settings,
    )(*args)


def held(*shape):
    return jax.ShapeDtypeStruct(shape, F32)


def exchange(x, partner):
    slabs, energies = lax.axis_size("slab"), lax.axis_size("energy")
    pairs = []
    for slab in range(slabs):
        for energy in range(energies):
            other = partner(energy)
            if 0 <= other < energies:
                target = slab * energies + other
            else:
                target = (slab ^ 1) % slabs * energies + energy
            pairs.append((slab * energies + energy, target))
    return lax.ppermute(x, ("slab", "energy"), pairs)


def in_pair(energy):
    return energy ^ 1


def in_one(energy):
    return energy ^ 2


def in_two(energy):
    return energy + 2 if energy // 2 % 2 == 1 else energy - 2


def per_device(
    onsite,
    hopping,
    separator_hamiltonian,
    coupling,
    bound_rows,
    old_sigma,
    phonon_vertex,
    mode_steps,
    mode_weights,
):
    size, few = hopping.shape[-1], coupling.shape[-1]
    energies, slabs = lax.axis_size("energy"), lax.axis_size("slab")
    assert energies % 2 == 0 and slabs & (slabs - 1) == 0
    half = size // 2
    cube = 3 * 8 * size**3
    full = held(size, 2 * size)
    sigma = old_sigma.reshape(2, size, size)
    mode_steps = mode_steps[None]
    given = [
        pltpu.with_memory_space_constraint(x, pltpu.HBM)
        for x in (onsite, hopping[0], sigma, coupling, bound_rows)
    ]
    first, second, start, rows, term = call(
        bound_kernel,
        [full, full, held(size, 2), held(few, 2 * size), held(few, 2 * few)],
        given,
        flops=2 * cube,
        in_specs=[pl.BlockSpec(memory_space=pltpu.HBM)] * len(given),
        scratch_shapes=[pltpu.VMEM(x.shape, x.dtype) for x in given]
        + [pltpu.SemaphoreType.DMA((len(given),))],
    )
    partial, left_side, right_side = call(
        power_kernel,
        [
            full,
            jax.ShapeDtypeStruct((size, 4 * size), BF16),
            jax.ShapeDtypeStruct((4 * size, 2 * size), BF16),
        ],
        [first, second, start],
        flops=2 * cube,
    )
    near, far, reach = term, None, slabs // 2
    while reach:
        if far is not None:
            far, partial = lax.optimization_barrier((far, partial))
            near = near + far
        far = lax.ppermute(near, "slab", [(i, i ^ reach) for i in range(slabs)])
        reach //= 2
    inverse = call(slab_kernel, full, [partial, left_side, right_side], flops=cube)
    part = held(half, size)
    middle, *greens = call(
        green_kernel,
        [held(size, 2 * few), part, part],
        [separator_hamiltonian, coupling, bound_rows, inverse, rows, near, far],
        flops=cube,
    )
    parts = []
    for at in (0, 1):
        green_a, green_b = greens
        two_a = exchange(green_a, in_two)
        one_a = exchange(green_a, in_one)
        pair_b = exchange(green_b, in_pair)
        parts.append((green_a, green_b, one_a, two_a, pair_b))
        if at == 0:
            greens = call(imaginary_kernel, [part, part], [middle, rows, inverse], flops=cube // 4)
    combined = []
    for part in parts:
        across_a, one_b, two_b = call(
            combine_kernel, [held(half, size)] * 3, [mode_steps, mode_weights, *part]
        )
        two_b = exchange(two_b, in_two)
        one_b = exchange(one_b, in_one)
        across_a = exchange(across_a, in_pair)
        combined.append((across_a, one_b, two_b))
    left = call(
        vertex_left_kernel, jax.ShapeDtypeStruct((size, 3 * size), BF16), [phonon_vertex[0]]
    )
    right = call(
        vertex_right_kernel, jax.ShapeDtypeStruct((3 * size, size), BF16), [phonon_vertex[0]]
    )
    out = None
    for at, (part, more) in enumerate(zip(parts, combined)):
        _, _, one_a, two_a, pair_b = part
        across_a, one_b, two_b = more
        args = [mode_steps, mode_weights, left, right, one_a, two_a, across_a, one_b, two_b, pair_b]
        vmem = pl.BlockSpec(memory_space=pltpu.VMEM)
        specs = [vmem] * len(args)
        aliases = {}
        if out is not None:
            aliases = {len(args): 0}
            args, specs = [*args, out], [*specs, pl.BlockSpec(memory_space=pl.ANY)]
        out = call(
            functools.partial(dress_kernel, at),
            held(2, size, size),
            args,
            flops=cube // 4,
            in_specs=specs,
            out_specs=pl.BlockSpec(memory_space=pl.ANY),
            scratch_shapes=[pltpu.VMEM((size, size), F32), pltpu.SemaphoreType.DMA((2,))],
            input_output_aliases=aliases,
        )
    return out.reshape(old_sigma.shape)


def solution(mesh):
    placed = (
        P("slab", None),
        P("slab", None, None),
        P(),
        P("slab", None),
        P("slab", None),
        P(None, "energy", "slab", None, None),
        P("slab", None, None),
        P(),
        P(),
    )

    return jax.shard_map(
        per_device,
        mesh=mesh,
        in_specs=placed,
        out_specs=P(None, "energy", "slab", None, None),
        check_vma=False,
    )
```
